32 devices in a mesh: groups: 2 (over x), blk: 16 (over z, y, core).
Axes of the slice: x: 2, y: 2, z: 4, core: 2. Of those that a mesh axis runs over, the one named last changes fastest.
Arguments:
- queries: bfloat16 [16384, 1536], P(('groups', 'blk')), parts along dimension 0, may hold values from -8 to 8
- key_rows: bfloat16 [16384, 1536], P(('groups', 'blk')), parts along dimension 0, may hold values from -8 to 8
- value_rows: bfloat16 [16384, 1536], P(('groups', 'blk')), parts along dimension 0, may hold values from -24 to 24
- block_mask: int32 [64, 20], P('blk'), may hold values from 0 to 1, as said below
- out_weight: bfloat16 [1536, 3072], P(None, 'blk'), may hold values from -0.5 to 0.5
Outputs:
- projected: bfloat16 [16384, 3072], P(('groups', 'blk')), parts along dimension 0
The draws below stay inside these ranges and needn't reach their ends.
There are 2 independent parts, one for each index of `groups`. The reference program is written for one: setup_inputs(seed, part) draws one part's arguments, and reference() takes and returns one part's arrays. A program takes and returns all parts, laid end to end along the dimension named above; an argument that names none is the same for every part. Nothing has to cross between parts.
Inputs may be any that keep to these rules, and one draw needn't show every extreme that they name: `block_mask`: entry [b, (d + 2) * 4 + j] is 1 if query block b may attend key block j of the slab d slabs after its own in cyclic order (before it for negative d). A slab's own blocks are always admitted. For d = 2 and d = -2, the query blocks of one slab together admit exactly 2 of that slab's key blocks, in every draw.
All inputs are finite; a program needn't handle non-finite values.
Results may differ from the reference program's by a relative error of at most 0.009.
Values may be sent and summed in bfloat16 or wider, within the bound.
A program may use at most 192 MiB of HBM per device.

```python
import math
import jax
import jax.numpy as jnp
from jax import lax

HEADS = 12
HD = 128
D = 3072
TOK_DEV = 512
BLOCK = 128
RADIUS = 2
BPD = 4
WIN = 5
FAR = 2
TOKENS = 8192
NBLK = 64
N_BLK = 16


def drawn_values(key):
    return jnp.clip(jax.random.normal(key, (TOKENS, HEADS * HD), jnp.float32), -6.0, 6.0)


def draw_queries(key, part):
    result = drawn_values(jax.random.fold_in(key, 1))
    return result.astype(jnp.bfloat16)


def draw_key_rows(key, part):
    result = drawn_values(jax.random.fold_in(key, 2))
    return result.astype(jnp.bfloat16)


def draw_block_mask(key, part):
    slab_count = NBLK // BPD
    col_count = WIN * BPD
    coin_toss = jax.random.randint(jax.random.fold_in(key, 3), (NBLK, col_count), 0, 4)
    col_index = jnp.arange(col_count)
    offset = col_index // BPD - RADIUS
    inner_block = col_index % BPD
    rank_key = jax.random.randint(jax.random.fold_in(key, 4), (slab_count, col_count), 0, 1 << 20) * BPD + inner_block[None, :]
    same_side = offset[:, None] == offset[None, :]
    smaller = (rank_key[:, None, :] < rank_key[:, :, None]) & same_side[None, :, :]
    position = jnp.sum(smaller.astype(jnp.int32), axis=2)
    allowed = position < FAR
    forced = jax.random.randint(jax.random.fold_in(key, 5), (slab_count, col_count), 0, BPD)
    row_slab = jnp.arange(NBLK) // BPD
    row_pos = jnp.arange(NBLK) % BPD
    far_bit = ((coin_toss > 0) | (row_pos[:, None] == forced[row_slab])) & allowed[row_slab]
    near_bit = coin_toss >= 2
    chosen_mask = jnp.where(offset[None, :] == 0, True, jnp.where(jnp.abs(offset)[None, :] == RADIUS, far_bit, near_bit))
    return chosen_mask.astype(jnp.int32)


def level_of(key, shape, split, least, high):
    loudness, own = 1.0, jax.random.fold_in(key, 6)
    for dim, parts in split:
        draws = jnp.exp(jax.random.uniform(jax.random.fold_in(own, dim), (parts,), jnp.float32, least / len(split), high / len(split)))
        loudness = loudness * jnp.repeat(draws, shape[dim] // parts).reshape([-1 if axis == dim else 1 for axis in range(len(shape))])
    return loudness


def centred(key, dims, width, reach, cuts=(), kind=jnp.bfloat16):
    values = width * jax.random.normal(key, dims, jnp.float32)
    if cuts:
        values = values * level_of(key, dims, cuts, -0.22, 0.18)
    return jnp.clip(values, -reach, reach).astype(kind)


def setup_inputs(seed: int = 0, part: int = 0) -> dict:
    key_of = jax.random.split(jax.random.key(seed), 6)
    own_keys = jax.random.split(jax.random.fold_in(key_of[5], part), 6)
    return {
        "queries": draw_queries(jax.random.fold_in(jax.random.fold_in(key_of[5], part), 71), part),
        "key_rows": draw_key_rows(jax.random.fold_in(jax.random.fold_in(key_of[5], part), 71), part),
        "value_rows": centred(own_keys[2], (TOKENS, HEADS * HD), 4.0, 24.0, ((0, 16),)),
        "block_mask": draw_block_mask(jax.random.fold_in(key_of[5], 71), part),
        "out_weight": centred(key_of[4], (HEADS * HD, D), HD ** -0.5, 0.5, ((1, 16),)),
    }


neg_large = -1e+30

def one_slab(slab, queries, key_rows, value_rows, block_mask, out_weight):
    feat_width = HEADS * HD
    first_row = (slab * TOK_DEV).astype(jnp.int32)
    query_heads = lax.dynamic_slice_in_dim(queries, first_row, TOK_DEV, 0).astype(jnp.float32).reshape(TOK_DEV, HEADS, HD)
    key_parts = []
    value_parts = []
    for offset in range(-RADIUS, RADIUS + 1):
        source = ((slab + offset) % N_BLK * TOK_DEV).astype(jnp.int32)
        key_parts.append(lax.dynamic_slice_in_dim(key_rows, source, TOK_DEV, 0))
        value_parts.append(lax.dynamic_slice_in_dim(value_rows, source, TOK_DEV, 0))
    key_heads = jnp.concatenate(key_parts, axis=0).astype(jnp.float32).reshape(WIN * TOK_DEV, HEADS, HD)
    value_heads = jnp.concatenate(value_parts, axis=0).astype(jnp.float32).reshape(WIN * TOK_DEV, HEADS, HD)
    mask_rows = lax.dynamic_slice_in_dim(block_mask, (slab * BPD).astype(jnp.int32), BPD, 0)
    keeping = (mask_rows > 0)[None, :, None, :, None]
    scores = jnp.einsum('qhe,khe->hqk', query_heads, key_heads, precision=lax.Precision.HIGHEST) * (1.0 / math.sqrt(HD))
    shaped = jnp.where(keeping, scores.reshape(HEADS, BPD, BLOCK, WIN * BPD, BLOCK), neg_large)
    top_score = lax.optimization_barrier(jnp.max(shaped, axis=(3, 4), keepdims=True))
    weights = jnp.where(keeping, jnp.exp(shaped - top_score), 0.0)
    total = lax.optimization_barrier(jnp.sum(weights, axis=(3, 4))).reshape(HEADS, TOK_DEV)
    rounded = lax.optimization_barrier(weights.reshape(HEADS, TOK_DEV, WIN * TOK_DEV).astype(jnp.bfloat16))
    summed = jnp.einsum('hqk,khe->qhe', rounded.astype(jnp.float32), value_heads, precision=lax.Precision.HIGHEST)
    attention = (summed / jnp.transpose(total)[:, :, None]).reshape(TOK_DEV, feat_width).astype(jnp.bfloat16)
    return jnp.dot(attention, out_weight, preferred_element_type=jnp.float32).astype(jnp.bfloat16)

def reference(queries, key_rows, value_rows, block_mask, out_weight):

    def per_slab(slab):
        return one_slab(slab, queries, key_rows, value_rows, block_mask, out_weight)
    stacked = lax.map(per_slab, jnp.arange(N_BLK, dtype=jnp.int32))
    return stacked.reshape(TOKENS, D)
```

```python
import functools
import math

import jax
import jax.numpy as jnp
from jax import lax
from jax.experimental import pallas as pl
from jax.experimental.pallas import tpu as pltpu
from jax.sharding import PartitionSpec as P

HEADS = 12
BLOCK = 128
RADIUS = 2
NEG = -1e30
OWN, ACROSS, ALONG, SIBLING, RELAYED = range(5)
MESH = pl.DeviceIdType.MESH


def nt_dot(a, b):
    return lax.dot_general(a, b, (((1,), (1,)), ((), ())), preferred_element_type=jnp.float32)


LOOKAHEAD = 4

def fused_kernel(
    q_hbm, k_hbm, v_hbm, mask_hbm, w_hbm, out_ref,
    q_buf, kv_buf, far_buf, fwd_buf, score_buf, heads_ref, w_buf, mask_buf, bias_buf, note_out, note_in,
    send_sem, recv_sem, load_sem, small_sem, note_sem,
    wz_send, wz_recv, wy_send, wy_recv, wx_send, wx_recv, ws_send, ws_recv,
):
    tok, feat = q_hbm.shape
    head = feat // HEADS
    rows = min(256, tok)
    blocks = rows // BLOCK
    per_slab = tok // BLOCK
    factor = math.log2(math.e) / math.sqrt(head)
    slabs = 16
    s = lax.axis_index("blk")
    g = lax.axis_index("groups")
    c = lax.rem(s, 2)
    y = lax.rem(s // 2, 2)
    z = s // 4
    sibling = s + 1 - 2 * c
    across = s + 2 - 4 * y
    along_to = lax.rem(s + 4 - 8 * y + slabs, slabs)
    along_from = lax.rem(s - 4 + 8 * y + slabs, slabs)
    late = lax.rem(y + c, 2)
    inward = jnp.where(z < 2, 1, -1)
    middle = jnp.where((z == 1) | (z == 2), 1, 0)
    inner = s + 4 * inward
    outer = s - 4 * inward

    def row_of(k):
        back = 0 if k == 0 else 2 if k == 1 else 1
        return z + inward * (k - middle * back)

    def cols(h):
        return pl.ds(pl.multiple_of(h * head, head), head)

    def load(h, which):
        src = (k_hbm, v_hbm, q_hbm)[which]
        dst = q_buf.at[h] if which == 2 else kv_buf.at[OWN, which, h]
        return pltpu.make_async_copy(src.at[:, cols(h)], dst, load_sem.at[h, which])

    def send(kind, h, which, source, place, target):
        return pltpu.make_async_remote_copy(
            src_ref=source,
            dst_ref=place,
            send_sem=send_sem.at[kind - 1, h, which],
            recv_sem=recv_sem.at[kind - 1, h, which],
            device_id={"blk": target},
            device_id_type=MESH,
        )

    def own_send(kind, h, which, target):
        return send(kind, h, which, (k_hbm, v_hbm)[which].at[:, cols(h)], kv_buf.at[kind, which, h], target)

    def pass_on(kind, held, h, which, target):
        return send(kind, h, which, kv_buf.at[held, which, h], kv_buf.at[kind, which, h], target)

    def far_send(h, which):
        return send(ALONG, h, which, fwd_buf.at[which, h], far_buf.at[1, which, h], along_to)

    def wait_for(kind, h, which):
        own_send(kind, h, which, sibling).wait_recv()

    width = w_hbm.shape[0]
    half = width // 2

    def w_place(r, col, core, part):
        index = 4 * r + 2 * col + core
        return pl.ds(pl.multiple_of(index * width + part * half, 32), half)

    def w_copy(source, place, sems, device):
        return pltpu.make_async_remote_copy(
            src_ref=source,
            dst_ref=w_buf.at[place],
            send_sem=sems[0],
            recv_sem=sems[1],
            device_id=device,
            device_id_type=MESH,
        )

    own_half = w_hbm.at[pl.ds(pl.multiple_of(g * half, 32), half)]

    def column(rel):
        return y if rel == 0 else 1 - y

    def w_z(rel, r, way, own=False):
        place = w_place(r, column(rel), c, g)
        return w_copy(
            own_half if own else w_buf.at[place], place,
            (wz_send.at[rel, r, way], wz_recv.at[rel, r]),
            {"blk": outer if way else inner},
        )

    def w_y(r, own=False):
        place = w_place(r, y, c, g)
        return w_copy(
            own_half if own else w_buf.at[place], place,
            (wy_send.at[r], wy_recv.at[r]), {"blk": across},
        )

    def w_x(rel, r, part):
        place = w_place(r, column(rel), c, part)
        return w_copy(
            w_buf.at[place], place, (wx_send.at[rel, r], wx_recv.at[rel, r]), {"groups": 1 - g}
        )

    def w_s(rel, r, part, own=False):
        place = w_place(r, column(rel), c, part)
        source = w_hbm.at[pl.ds(pl.multiple_of(part * half, 32), half)] if own else w_buf.at[place]
        return w_copy(
            source, place, (ws_send.at[part, rel, r], ws_recv.at[part, rel, r]), {"blk": sibling}
        )

    own_place = pl.ds(pl.multiple_of(s * width, 32), width)
    w_keep = pltpu.make_async_copy(w_hbm, w_buf.at[own_place], small_sem.at[1])
    mask_load = pltpu.make_async_copy(mask_hbm, mask_buf, small_sem.at[0])
    note = pltpu.make_async_remote_copy(
        src_ref=note_out,
        dst_ref=note_in,
        send_sem=note_sem.at[0],
        recv_sem=note_sem.at[1],
        device_id={"blk": along_from},
        device_id_type=MESH,
    )

    mask_load.start()
    barrier = pltpu.get_barrier_semaphore()
    peers = [{"blk": device} for device in (sibling, across, along_to, along_from)]
    peers.append({"groups": 1 - g})
    for device in peers:
        pl.semaphore_signal(barrier, inc=1, device_id=device, device_id_type=MESH)
    pl.semaphore_wait(barrier, len(peers))

    def begin_across(h, carry):
        for which in range(2):
            own_send(ACROSS, h, which, across).start()
        return carry

    def begin(h, carry):
        for which in range(2):
            own_send(SIBLING, h, which, sibling).start()
        for which in range(3):
            load(h, which).start()
        return carry

    begin_across(0, 0)
    w_z(0, z, 0, own=True).start()

    @pl.when(middle == 1)
    def _():
        w_z(0, z, 1, own=True).start()

    begin_across(1, 0)

    @pl.when(c == 0)
    def _():
        w_y(z, own=True).start()

    lax.fori_loop(2, LOOKAHEAD, begin_across, 0)
    lax.fori_loop(0, HEADS, begin, 0)
    w_keep.start()
    for part in range(2):
        w_s(0, z, part, own=True).start()

    mask_load.wait()
    base_across = jnp.where(y == 0, 4 * per_slab, 0)
    base_along = 4 * per_slab - base_across
    base_sibling = jnp.where(c == 0, 3 * per_slab, per_slab)
    base_relayed = 4 * per_slab - base_sibling

    def admitted(base):
        used = []
        for n in range(per_slab):
            value = mask_buf[0, base + n]
            for b in range(1, per_slab):
                value = jnp.maximum(value, mask_buf[b, base + n])
            used.append(value > 0)
        first = jnp.where(used[0], 0, jnp.where(used[1], 1, 2))
        second = jnp.where(used[3], 3, jnp.where(used[2], 2, 1))
        return first, second

    across_pick = admitted(base_across)
    along_pick = admitted(base_along)
    for n in range(2):
        level = jnp.full(note_out.shape[1:], along_pick[n].astype(jnp.float32), jnp.float32)
        note_out[n] = level.astype(jnp.bfloat16)
    note.start()

    def offset(value):
        return jnp.where(value > 0, 0.0, NEG).astype(jnp.float32)

    for b in range(per_slab):
        for n in range(per_slab):
            bias_buf[b, n] = offset(mask_buf[b, base_sibling + n])
            bias_buf[b, per_slab + n] = offset(mask_buf[b, base_relayed + n])
        for n in range(2):
            bias_buf[b, 2 * per_slab + n] = offset(mask_buf[b, base_across + across_pick[n]])
            bias_buf[b, 2 * per_slab + 2 + n] = offset(mask_buf[b, base_along + along_pick[n]])
    note.wait()

    def gather_far(kind, held, h, which, picks):
        piece = [kv_buf[held, which, h, n * BLOCK : (n + 1) * BLOCK, :] for n in range(per_slab)]
        first = lax.select(picks[0] == 0, piece[0], lax.select(picks[0] == 1, piece[1], piece[2]))
        second = lax.select(picks[1] == 3, piece[3], lax.select(picks[1] == 2, piece[2], piece[1]))
        far_buf[kind, which, h, :BLOCK, :] = first
        far_buf[kind, which, h, BLOCK:, :] = second

    def gather_forward(h, which):
        size = note_in.shape[1]
        first, second = note_in[0], note_in[1]
        for t in range(BLOCK // size):
            piece = [
                kv_buf[ACROSS, which, h, n * BLOCK + t * size : n * BLOCK + (t + 1) * size, :]
                for n in range(per_slab)
            ]
            fwd_buf[which, h, t * size : (t + 1) * size, :] = jnp.where(
                first == 0, piece[0], jnp.where(first == 1, piece[1], piece[2])
            )
            fwd_buf[which, h, BLOCK + t * size : BLOCK + (t + 1) * size, :] = jnp.where(
                second == 3, piece[3], jnp.where(second == 2, piece[2], piece[1])
            )

    def head_rows(h, part):
        first = pl.multiple_of(part * rows, rows)
        q = q_buf[h, pl.ds(first, rows), :]
        segments = [
            (kv_buf.at[OWN], tok, None),
            (kv_buf.at[SIBLING], tok, 0),
            (kv_buf.at[RELAYED], tok, per_slab),
            (far_buf.at[0], 2 * BLOCK, 2 * per_slab),
            (far_buf.at[1], 2 * BLOCK, 2 * per_slab + 2),
        ]
        peak = jnp.full((rows, BLOCK), NEG, jnp.float32)
        start = 0
        for ref, length, bias in segments:
            raw = nt_dot(q, ref[0, h]) * factor
            for n in range(length // BLOCK):
                col = start + n * BLOCK
                for b in range(blocks):
                    piece = raw[b * BLOCK : (b + 1) * BLOCK, n * BLOCK : (n + 1) * BLOCK]
                    if bias is not None:
                        piece = piece + bias_buf[part * blocks + b, bias + n]
                    score_buf[b * BLOCK : (b + 1) * BLOCK, col : col + BLOCK] = piece
                peak = jnp.maximum(peak, score_buf[:, col : col + BLOCK])
            start += length
        top = jnp.max(peak, axis=1, keepdims=True)
        mass = jnp.zeros((rows, BLOCK), jnp.float32)
        total = jnp.zeros((rows, head), jnp.float32)
        start = 0
        for ref, length, bias in segments:
            weights = jnp.exp2(score_buf[:, start : start + length] - top)
            for n in range(length // BLOCK):
                mass = mass + weights[:, n * BLOCK : (n + 1) * BLOCK]
            total = total + jnp.dot(
                weights.astype(jnp.bfloat16), ref[1, h], preferred_element_type=jnp.float32
            )
            start += length
        result = total / jnp.sum(mass, axis=1, keepdims=True)
        heads_ref[pl.ds(first, rows), cols(h)] = result.astype(jnp.bfloat16)

    def compute(h):
        for which in range(3):
            load(h, which).wait()
        for which in range(2):
            wait_for(SIBLING, h, which)

        @pl.when(late == 0)
        def _():
            for which in range(2):
                far_send(h, which).wait_recv()

        for which in range(2):
            wait_for(RELAYED, h, which)

        def part_step(part, carry):
            head_rows(h, part)
            return carry

        lax.fori_loop(0, tok // rows, part_step, 0)

    def relay(h):
        for which in range(2):
            wait_for(ACROSS, h, which)

            @pl.when(late == 1)
            def _():
                pass_on(ALONG, ACROSS, h, which, along_to).start()

            @pl.when(late == 0)
            def _():
                gather_forward(h, which)
                far_send(h, which).start()
                pass_on(RELAYED, ACROSS, h, which, sibling).start()

            gather_far(0, ACROSS, h, which, across_pick)

    def relay_late(h):
        for which in range(2):
            wait_for(ALONG, h, which)
            pass_on(RELAYED, ALONG, h, which, sibling).start()
            gather_far(1, ALONG, h, which, along_pick)

    def got(rel, r):
        w_x(rel, r, g).start()
        w_s(rel, r, g).start()

    def z_arrives(k, rel):
        r = row_of(k)
        w_z(rel, r, 0).wait_recv()

        @pl.when(middle == 1)
        def _():
            w_z(rel, r, 0 if k == 1 else 1).start()

        got(rel, r)

    def twin_arrives(k, rel):
        r = row_of(k)
        w_x(rel, r, 1 - g).wait_recv()
        w_s(rel, r, 1 - g).start()

    def at(i, when, core=None):
        if core is None:
            return pl.when(i == when)
        return pl.when((i == when) & (c == core))

    def weight_step(i):
        @at(i, 1, 0)
        def _():
            w_y_wait_row(z)
            w_z(1, z, 0).start()

            @pl.when(middle == 1)
            def _():
                w_z(1, z, 1).start()

            got(1, z)

        for k, rel, when in ((1, 0, 2), (2, 0, 3), (3, 0, 5)):

            @at(i, when)
            def _():
                z_arrives(k, rel)

        for k, rel, when in ((1, 1, 3), (2, 1, 5), (3, 1, 7)):

            @at(i, when, 0)
            def _():
                z_arrives(k, rel)

        for k, rel, when in ((1, 0, 4), (2, 0, 5), (3, 0, 7)):

            @at(i, when)
            def _():
                twin_arrives(k, rel)

        for k, rel, when in ((0, 1, 3), (1, 1, 5), (2, 1, 7), (3, 1, 9)):

            @at(i, when, 0)
            def _():
                twin_arrives(k, rel)

        @at(i, 9, 1)
        def _():
            w_y(z, own=True).start()
            w_y(row_of(1)).start()

        @at(i, 10, 1)
        def _():
            w_y(row_of(2)).start()
            w_y(row_of(3)).start()

        @at(i, 12, 1)
        def _():
            across_arrives(0)

        @at(i, 13, 1)
        def _():
            across_arrives(1)

    def w_y_wait_row(r):
        place = w_place(r, 1 - y, c, g)
        w_copy(
            w_buf.at[place], w_place(r, 1 - y, c, g), (wy_send.at[r], wy_recv.at[r]), {"blk": across}
        ).wait_recv()

    def across_arrives(k):
        r = row_of(k)
        w_y_wait_row(r)
        got(1, r)

    def step(i, carry):
        @pl.when((i >= 2) & (i < HEADS))
        def _():
            compute(i - 2)

        @pl.when(i < HEADS)
        def _():
            relay(i)

        @pl.when(i + LOOKAHEAD < HEADS)
        def _():
            begin_across(i + LOOKAHEAD, 0)

        @pl.when((i >= 1) & (i < HEADS + 1) & (late == 1))
        def _():
            relay_late(i - 1)

        weight_step(i)

        @pl.when(i >= HEADS)
        def _():
            compute(i - 2)

        return carry

    lax.fori_loop(0, HEADS + 2, step, 0)

    @pl.when(c == 1)
    def _():
        across_arrives(2)
        across_arrives(3)

    w_keep.wait()
    chunk = 2 * width
    for k in range(4):
        r = row_of(k)

        @pl.when(c == 1)
        def _():
            twin_arrives(k, 1)

        for rel in range(2):
            for part in range(2):
                place = w_place(r, column(rel), 1 - c, part)
                w_copy(
                    w_buf.at[place], place,
                    (ws_send.at[part, rel, r], ws_recv.at[part, rel, r]), {"blk": sibling},
                ).wait_recv()

        def tile(t, carry):
            place = pl.ds(pl.multiple_of((2 * r + t) * chunk, 128), chunk)
            out_ref[:, place] = nt_dot(heads_ref[...], w_buf[place, :]).astype(out_ref.dtype)
            return carry

        lax.fori_loop(0, 2, tile, 0)

    def finish(h, carry):
        for kind in (ACROSS, SIBLING, RELAYED):
            for which in range(2):
                own_send(kind, h, which, sibling).wait_send()

        @pl.when(late == 1)
        def _():
            for which in range(2):
                own_send(ALONG, h, which, sibling).wait_send()

        @pl.when(late == 0)
        def _():
            for which in range(2):
                far_send(h, which).wait_send()

        return carry

    lax.fori_loop(0, HEADS, finish, 0)

    def z_sent(rel):
        w_z(rel, z, 0).wait_send()

        @pl.when(middle == 1)
        def _():
            w_z(rel, z, 1).wait_send()
            w_z(rel, row_of(1), 0).wait_send()
            w_z(rel, row_of(2), 1).wait_send()
            w_z(rel, row_of(3), 1).wait_send()

    z_sent(0)

    @pl.when(c == 0)
    def _():
        z_sent(1)
        w_y(z).wait_send()

    @pl.when(c == 1)
    def _():
        for k in range(4):
            w_y(row_of(k)).wait_send()

    for k in range(4):
        r = row_of(k)
        for rel in range(2):
            if k or rel:
                w_x(rel, r, g).wait_send()
            for part in range(2):
                w_s(rel, r, part).wait_send()


def fused(queries, key_rows, value_rows, block_mask, weight):
    tok, feat = queries.shape
    head = feat // HEADS
    width = 16 * weight.shape[0]
    per_slab = tok // BLOCK
    columns = 3 * tok + 4 * BLOCK
    dma = pltpu.SemaphoreType.DMA
    bf16, f32 = jnp.bfloat16, jnp.float32
    scratch = [
        pltpu.VMEM((HEADS, tok, head), bf16),
        pltpu.VMEM((5, 2, HEADS, tok, head), bf16),
        pltpu.VMEM((2, 2, HEADS, 2 * BLOCK, head), bf16),
        pltpu.VMEM((2, HEADS, 2 * BLOCK, head), bf16),
        pltpu.VMEM((min(256, tok), columns), f32),
        pltpu.VMEM((tok, feat), bf16),
        pltpu.VMEM((width, feat), bf16),
        pltpu.SMEM(block_mask.shape, jnp.int32),
        pltpu.SMEM((per_slab, 2 * per_slab + 4), f32),
        pltpu.VMEM((2, 16, head), bf16),
        pltpu.VMEM((2, 16, head), bf16),
        dma((4, HEADS, 2)),
        dma((4, HEADS, 2)),
        dma((HEADS, 3)),
        dma((2,)),
        dma((2,)),
        dma((2, 4, 2)),
        dma((2, 4)),
        dma((4,)),
        dma((4,)),
        dma((2, 4)),
        dma((2, 4)),
        dma((2, 2, 4)),
        dma((2, 2, 4)),
    ]
    return pl.pallas_call(
        fused_kernel,
        out_shape=jax.ShapeDtypeStruct((tok, width), bf16),
        in_specs=[pl.BlockSpec(memory_space=pl.ANY)] * 5,
        out_specs=pl.BlockSpec(memory_space=pltpu.VMEM),
        scratch_shapes=scratch,
        compiler_params=pltpu.CompilerParams(
            collective_id=0, has_side_effects=True, vmem_limit_bytes=60 * 2**20
        ),
    )(queries, key_rows, value_rows, block_mask, weight)


def attend_kernel(slabs, q_hbm, k_hbm, v_hbm, bias_ref, heads_ref, q_buf, kv_buf, score_buf, send_sem, recv_sem, load_sem):
    tok, feat = q_hbm.shape
    head = feat // HEADS
    rows = min(256, tok)
    blocks = rows // BLOCK
    factor = math.log2(math.e) / math.sqrt(head)
    s = lax.axis_index("blk")
    c = lax.rem(s, 2)
    y = lax.rem(s // 2, 2)
    sibling = s + 1 - 2 * c
    across = s + 2 - 4 * y
    along_to = lax.rem(s + 4 - 8 * y + slabs, slabs)
    along_from = lax.rem(s - 4 + 8 * y + slabs, slabs)
    late = lax.rem(y + c, 2)

    def cols(h):
        return pl.ds(pl.multiple_of(h * head, head), head)

    def load(h, which):
        src = (k_hbm, v_hbm, q_hbm)[which]
        dst = q_buf.at[h] if which == 2 else kv_buf.at[OWN, which, h]
        return pltpu.make_async_copy(src.at[:, cols(h)], dst, load_sem.at[h, which])

    def send(kind, h, which, source, target):
        return pltpu.make_async_remote_copy(
            src_ref=source,
            dst_ref=kv_buf.at[kind, which, h],
            send_sem=send_sem.at[kind - 1, h, which],
            recv_sem=recv_sem.at[kind - 1, h, which],
            device_id={"blk": target},
            device_id_type=MESH,
        )

    def own_send(kind, h, which, target):
        return send(kind, h, which, (k_hbm, v_hbm)[which].at[:, cols(h)], target)

    def pass_on(kind, held, h, which, target):
        return send(kind, h, which, kv_buf.at[held, which, h], target)

    def wait_for(kind, h, which):
        own_send(kind, h, which, sibling).wait_recv()

    def arrived(kind, h):
        for which in range(2):
            wait_for(kind, h, which)

    barrier = pltpu.get_barrier_semaphore()
    peers = (sibling, across, along_to, along_from)
    for device in peers:
        pl.semaphore_signal(barrier, inc=1, device_id={"blk": device}, device_id_type=MESH)
    pl.semaphore_wait(barrier, len(peers))

    def begin_across(h, carry):
        for which in range(2):
            own_send(ACROSS, h, which, across).start()
        return carry

    def begin(h, carry):
        for which in range(2):
            own_send(SIBLING, h, which, sibling).start()
        for which in range(3):
            load(h, which).start()
        return carry

    lax.fori_loop(0, LOOKAHEAD, begin_across, 0)
    lax.fori_loop(0, HEADS, begin, 0)

    def head_rows(h, part):
        first = pl.multiple_of(part * rows, rows)
        q = q_buf[h, pl.ds(first, rows), :]
        peak = jnp.full((rows, 128), NEG, jnp.float32)
        for j in range(5):
            raw = nt_dot(q, kv_buf[j, 0, h]) * factor
            for b in range(blocks):
                for n in range(tok // BLOCK):
                    col = j * tok + n * BLOCK
                    piece = raw[b * BLOCK : (b + 1) * BLOCK, n * BLOCK : (n + 1) * BLOCK]
                    piece = piece + bias_ref[part * blocks + b, :, col : col + BLOCK]
                    score_buf[b * BLOCK : (b + 1) * BLOCK, col : col + BLOCK] = piece
            for n in range(tok // BLOCK):
                col = j * tok + n * BLOCK
                peak = jnp.maximum(peak, score_buf[:, col : col + BLOCK])
        top = jnp.max(peak, axis=1, keepdims=True)
        mass = jnp.zeros((rows, 128), jnp.float32)
        total = jnp.zeros((rows, head), jnp.float32)
        for j in range(5):
            weights = jnp.exp2(score_buf[:, j * tok : (j + 1) * tok] - top)
            for n in range(tok // BLOCK):
                mass = mass + weights[:, n * BLOCK : (n + 1) * BLOCK]
            total = total + jnp.dot(
                weights.astype(jnp.bfloat16), kv_buf[j, 1, h], preferred_element_type=jnp.float32
            )
        result = total / jnp.sum(mass, axis=1, keepdims=True)
        heads_ref[pl.ds(first, rows), cols(h)] = result.astype(jnp.bfloat16)

    def compute(h):
        for which in range(3):
            load(h, which).wait()
        arrived(SIBLING, h)

        @pl.when(late == 0)
        def _():
            arrived(ALONG, h)

        arrived(RELAYED, h)

        def part_step(part, carry):
            head_rows(h, part)
            return carry

        lax.fori_loop(0, tok // rows, part_step, 0)

    def relay_late(h):
        for which in range(2):
            wait_for(ALONG, h, which)
            pass_on(RELAYED, ALONG, h, which, sibling).start()

    def step(i, carry):
        @pl.when((i >= 2) & (i < HEADS))
        def _():
            compute(i - 2)

        @pl.when(i < HEADS)
        def _():
            for which in range(2):
                wait_for(ACROSS, i, which)
                pass_on(ALONG, ACROSS, i, which, along_to).start()

                @pl.when(late == 0)
                def _():
                    pass_on(RELAYED, ACROSS, i, which, sibling).start()

        @pl.when(i + LOOKAHEAD < HEADS)
        def _():
            begin_across(i + LOOKAHEAD, 0)

        @pl.when((i >= 1) & (i < HEADS + 1) & (late == 1))
        def _():
            relay_late(i - 1)

        @pl.when(i >= HEADS)
        def _():
            compute(i - 2)

        return carry

    lax.fori_loop(0, HEADS + 2, step, 0)

    def finish(h, carry):
        for kind in (ACROSS, ALONG, SIBLING, RELAYED):
            for which in range(2):
                own_send(kind, h, which, sibling).wait_send()
        return carry

    lax.fori_loop(0, HEADS, finish, 0)


def attend(slabs, queries, key_rows, value_rows, bias):
    tok, feat = queries.shape
    head = feat // HEADS
    return pl.pallas_call(
        functools.partial(attend_kernel, slabs),
        out_shape=jax.ShapeDtypeStruct((tok, feat), jnp.bfloat16),
        in_specs=[pl.BlockSpec(memory_space=pl.ANY)] * 3 + [pl.BlockSpec(memory_space=pltpu.VMEM)],
        out_specs=pl.BlockSpec(memory_space=pltpu.VMEM),
        scratch_shapes=[
            pltpu.VMEM((HEADS, tok, head), jnp.bfloat16),
            pltpu.VMEM((5, 2, HEADS, tok, head), jnp.bfloat16),
            pltpu.VMEM((min(256, tok), 5 * tok), jnp.float32),
            pltpu.SemaphoreType.DMA((4, HEADS, 2)),
            pltpu.SemaphoreType.DMA((4, HEADS, 2)),
            pltpu.SemaphoreType.DMA((HEADS, 3)),
        ],
        compiler_params=pltpu.CompilerParams(
            collective_id=0, has_side_effects=True, vmem_limit_bytes=60 * 2**20
        ),
    )(queries, key_rows, value_rows, bias)


def local(slabs, groups, queries, key_rows, value_rows, block_mask, out_weight):
    per_slab = queries.shape[0] // BLOCK
    if groups == 2 and slabs == 16 and per_slab == 4 and out_weight.shape[1] % 64 == 0:
        return fused(queries, key_rows, value_rows, block_mask, out_weight.T)
    s = lax.axis_index("blk")
    c = s % 2
    y = (s // 2) % 2
    table = jnp.where(block_mask > 0, 0.0, NEG).astype(jnp.float32)
    table = table.reshape(block_mask.shape[0], 2 * RADIUS + 1, per_slab)
    back2, back1, own, next1, next2 = (table[:, d] for d in range(5))
    ordered = jnp.concatenate(
        (
            own,
            jnp.where(y == 0, next2, back2),
            jnp.where(y == 0, back2, next2),
            jnp.where(c == 0, next1, back1),
            jnp.where(c == 0, back1, next1),
        ),
        axis=1,
    )
    bias = jnp.repeat(ordered, BLOCK, axis=1)[:, None, :]
    attention = attend(slabs, queries, key_rows, value_rows, bias)
    weight = lax.all_gather(out_weight, "blk", axis=1, tiled=True)
    return jnp.dot(attention, weight, preferred_element_type=jnp.float32).astype(jnp.bfloat16)


def solution(mesh):
    in_specs = (
        P(("groups", "blk"), None),
        P(("groups", "blk"), None),
        P(("groups", "blk"), None),
        P("blk", None),
        P(None, "blk"),
    )
    out_specs = P(("groups", "blk"), None)
    body = functools.partial(local, mesh.shape["blk"], mesh.shape["groups"])
    return jax.shard_map(body, mesh=mesh, in_specs=in_specs, out_specs=out_specs, check_vma=False)
```

```python
import functools
import math

import jax
import jax.numpy as jnp
from jax import lax
from jax.experimental import pallas as pl
from jax.experimental.pallas import tpu as pltpu
from jax.sharding import PartitionSpec as P

HEADS = 12
BLOCK = 128
RADIUS = 2
NEG = -1e30
OWN, ACROSS, ALONG, SIBLING, RELAYED = range(5)
MESH = pl.DeviceIdType.MESH


def nt_dot(a, b):
    return lax.dot_general(a, b, (((1,), (1,)), ((), ())), preferred_element_type=jnp.float32)


LOOKAHEAD = 4
LAG = 3
SLICES = 3

def fused_kernel(
    q_hbm, k_hbm, v_hbm, mask_hbm, w_hbm, out_ref,
    q_buf, kv_buf, far_buf, fwd_buf, score_buf, heads_ref, w_buf, mask_buf, bias_buf, note_out, note_in,
    send_sem, recv_sem, load_sem, small_sem, note_sem,
    wz_send, wz_recv, wy_send, wy_recv, wx_send, wx_recv, ws_send, ws_recv,
    ty_send, ty_recv, tx_send, tx_recv, ts_send, ts_recv,
):
    tok, feat = q_hbm.shape
    head = feat // HEADS
    rows = min(256, tok)
    blocks = rows // BLOCK
    per_slab = tok // BLOCK
    factor = math.log2(math.e) / math.sqrt(head)
    slabs = 16
    s = lax.axis_index("blk")
    g = lax.axis_index("groups")
    c = lax.rem(s, 2)
    y = lax.rem(s // 2, 2)
    z = s // 4
    sibling = s + 1 - 2 * c
    across = s + 2 - 4 * y
    along_to = lax.rem(s + 4 - 8 * y + slabs, slabs)
    along_from = lax.rem(s - 4 + 8 * y + slabs, slabs)
    late = lax.rem(y + c, 2)
    inward = jnp.where(z < 2, 1, -1)
    middle = jnp.where((z == 1) | (z == 2), 1, 0)
    inner = s + 4 * inward
    outer = s - 4 * inward

    def row_of(k):
        back = 0 if k == 0 else 2 if k == 1 else 1
        return z + inward * (k - middle * back)

    def cols(h):
        return pl.ds(pl.multiple_of(h * head, head), head)

    def load(h, which):
        src = (k_hbm, v_hbm, q_hbm)[which]
        dst = q_buf.at[h] if which == 2 else kv_buf.at[OWN, which, h]
        return pltpu.make_async_copy(src.at[:, cols(h)], dst, load_sem.at[h, which])

    def send(kind, h, which, source, place, target):
        return pltpu.make_async_remote_copy(
            src_ref=source,
            dst_ref=place,
            send_sem=send_sem.at[kind - 1, h, which],
            recv_sem=recv_sem.at[kind - 1, h, which],
            device_id={"blk": target},
            device_id_type=MESH,
        )

    def own_send(kind, h, which, target):
        return send(kind, h, which, (k_hbm, v_hbm)[which].at[:, cols(h)], kv_buf.at[kind, which, h], target)

    def pass_on(kind, held, h, which, target):
        return send(kind, h, which, kv_buf.at[held, which, h], kv_buf.at[kind, which, h], target)

    def far_send(h, which):
        return send(ALONG, h, which, fwd_buf.at[which, h], far_buf.at[1, which, h], along_to)

    def wait_for(kind, h, which):
        pass_on(kind, kind, h, which, sibling).wait_recv()

    width = w_hbm.shape[0]
    half = width // 2

    def w_place(r, col, core, part):
        index = 4 * r + 2 * col + core
        return pl.ds(pl.multiple_of(index * width + part * half, 32), half)

    def w_copy(source, place, sems, device):
        return pltpu.make_async_remote_copy(
            src_ref=source,
            dst_ref=w_buf.at[place],
            send_sem=sems[0],
            recv_sem=sems[1],
            device_id=device,
            device_id_type=MESH,
        )

    own_half = w_hbm.at[pl.ds(pl.multiple_of(g * half, 32), half)]

    def column(rel):
        return y if rel == 0 else 1 - y

    def w_z(rel, r, way, own=False):
        place = w_place(r, column(rel), c, g)
        return w_copy(
            own_half if own else w_buf.at[place], place,
            (wz_send.at[rel, r, way], wz_recv.at[rel, r]),
            {"blk": outer if way else inner},
        )

    def w_y(r, own=False):
        place = w_place(r, y, c, g)
        return w_copy(
            own_half if own else w_buf.at[place], place,
            (wy_send.at[r], wy_recv.at[r]), {"blk": across},
        )

    thin = half // SLICES

    def slice_rows(start, q):
        return pl.ds(pl.multiple_of(start + q * thin, 32), thin)

    def slice_place(r, col, part, q):
        return slice_rows((4 * r + 2 * col + 1) * width + part * half, q)

    def t_y(r, q, own=False):
        place = slice_place(r, y, g, q)
        return w_copy(
            w_hbm.at[slice_rows(g * half, q)] if own else w_buf.at[place], place,
            (ty_send.at[r, q], ty_recv.at[r, q]), {"blk": across},
        )

    def t_y_wait(r, q):
        place = slice_place(r, 1 - y, g, q)
        w_copy(w_buf.at[place], place, (ty_send.at[r, q], ty_recv.at[r, q]), {"blk": across}).wait_recv()

    def t_x(r, part, q):
        place = slice_place(r, 1 - y, part, q)
        return w_copy(w_buf.at[place], place, (tx_send.at[r, q], tx_recv.at[r, q]), {"groups": 1 - g})

    def t_s(r, part, q):
        place = slice_place(r, 1 - y, part, q)
        return w_copy(
            w_buf.at[place], place, (ts_send.at[part, r, q], ts_recv.at[part, r, q]), {"blk": sibling}
        )

    def w_x(rel, r, part):
        place = w_place(r, column(rel), c, part)
        return w_copy(
            w_buf.at[place], place, (wx_send.at[rel, r], wx_recv.at[rel, r]), {"groups": 1 - g}
        )

    def w_s(rel, r, part, own=False):
        place = w_place(r, column(rel), c, part)
        source = w_hbm.at[pl.ds(pl.multiple_of(part * half, 32), half)] if own else w_buf.at[place]
        return w_copy(
            source, place, (ws_send.at[part, rel, r], ws_recv.at[part, rel, r]), {"blk": sibling}
        )

    own_place = pl.ds(pl.multiple_of(s * width, 32), width)
    w_keep = pltpu.make_async_copy(w_hbm, w_buf.at[own_place], small_sem.at[1])
    mask_load = pltpu.make_async_copy(mask_hbm, mask_buf, small_sem.at[0])
    note = pltpu.make_async_remote_copy(
        src_ref=note_out,
        dst_ref=note_in,
        send_sem=note_sem.at[0],
        recv_sem=note_sem.at[1],
        device_id={"blk": along_from},
        device_id_type=MESH,
    )

    mask_load.start()
    barrier = pltpu.get_barrier_semaphore()
    peers = [{"blk": device} for device in (sibling, across, along_to, along_from)]
    peers.append({"groups": 1 - g})
    for device in peers:
        pl.semaphore_signal(barrier, inc=1, device_id=device, device_id_type=MESH)
    pl.semaphore_wait(barrier, len(peers))

    def begin_across(h, carry):
        for which in range(2):
            own_send(ACROSS, h, which, across).start()
        return carry

    def begin(h, carry):
        for which in range(2):
            own_send(SIBLING, h, which, sibling).start()
        for which in range(3):
            load(h, which).start()
        return carry

    begin_across(0, 0)
    w_z(0, z, 0, own=True).start()

    @pl.when(middle == 1)
    def _():
        w_z(0, z, 1, own=True).start()

    begin_across(1, 0)

    @pl.when(c == 0)
    def _():
        w_y(z, own=True).start()

    lax.fori_loop(2, LOOKAHEAD, begin_across, 0)
    lax.fori_loop(0, HEADS, begin, 0)
    w_keep.start()
    for part in range(2):
        w_s(0, z, part, own=True).start()

    mask_load.wait()
    base_across = jnp.where(y == 0, 4 * per_slab, 0)
    base_along = 4 * per_slab - base_across
    base_sibling = jnp.where(c == 0, 3 * per_slab, per_slab)
    base_relayed = 4 * per_slab - base_sibling

    def admitted(base):
        used = []
        for n in range(per_slab):
            value = mask_buf[0, base + n]
            for b in range(1, per_slab):
                value = jnp.maximum(value, mask_buf[b, base + n])
            used.append(value > 0)
        first = jnp.where(used[0], 0, jnp.where(used[1], 1, 2))
        second = jnp.where(used[3], 3, jnp.where(used[2], 2, 1))
        return first, second

    across_pick = admitted(base_across)
    along_pick = admitted(base_along)
    for n in range(2):
        level = jnp.full(note_out.shape[1:], along_pick[n].astype(jnp.float32), jnp.float32)
        note_out[n] = level.astype(jnp.bfloat16)
    note.start()

    def offset(value):
        return jnp.where(value > 0, 0.0, NEG).astype(jnp.float32)

    for b in range(per_slab):
        for n in range(per_slab):
            bias_buf[b, n] = offset(mask_buf[b, base_sibling + n])
            bias_buf[b, per_slab + n] = offset(mask_buf[b, base_relayed + n])
        for n in range(2):
            bias_buf[b, 2 * per_slab + n] = offset(mask_buf[b, base_across + across_pick[n]])
            bias_buf[b, 2 * per_slab + 2 + n] = offset(mask_buf[b, base_along + along_pick[n]])
    note.wait()

    def gather_far(kind, held, h, which, picks):
        piece = [kv_buf[held, which, h, n * BLOCK : (n + 1) * BLOCK, :] for n in range(per_slab)]
        first = lax.select(picks[0] == 0, piece[0], lax.select(picks[0] == 1, piece[1], piece[2]))
        second = lax.select(picks[1] == 3, piece[3], lax.select(picks[1] == 2, piece[2], piece[1]))
        far_buf[kind, which, h, :BLOCK, :] = first
        far_buf[kind, which, h, BLOCK:, :] = second

    def gather_forward(h, which):
        size = note_in.shape[1]
        first, second = note_in[0], note_in[1]
        for t in range(BLOCK // size):
            piece = [
                kv_buf[ACROSS, which, h, n * BLOCK + t * size : n * BLOCK + (t + 1) * size, :]
                for n in range(per_slab)
            ]
            fwd_buf[which, h, t * size : (t + 1) * size, :] = jnp.where(
                first == 0, piece[0], jnp.where(first == 1, piece[1], piece[2])
            )
            fwd_buf[which, h, BLOCK + t * size : BLOCK + (t + 1) * size, :] = jnp.where(
                second == 3, piece[3], jnp.where(second == 2, piece[2], piece[1])
            )

    def head_rows(h, part):
        first = pl.multiple_of(part * rows, rows)
        q = q_buf[h, pl.ds(first, rows), :]
        segments = [
            (kv_buf.at[OWN], tok, None),
            (kv_buf.at[SIBLING], tok, 0),
            (kv_buf.at[RELAYED], tok, per_slab),
            (far_buf.at[0], 2 * BLOCK, 2 * per_slab),
            (far_buf.at[1], 2 * BLOCK, 2 * per_slab + 2),
        ]
        peak = jnp.full((rows, BLOCK), NEG, jnp.float32)
        start = 0
        for ref, length, bias in segments:
            raw = nt_dot(q, ref[0, h]) * factor
            for n in range(length // BLOCK):
                col = start + n * BLOCK
                for b in range(blocks):
                    piece = raw[b * BLOCK : (b + 1) * BLOCK, n * BLOCK : (n + 1) * BLOCK]
                    if bias is not None:
                        piece = piece + bias_buf[part * blocks + b, bias + n]
                    score_buf[b * BLOCK : (b + 1) * BLOCK, col : col + BLOCK] = piece
                peak = jnp.maximum(peak, score_buf[:, col : col + BLOCK])
            start += length
        top = jnp.max(peak, axis=1, keepdims=True)
        mass = jnp.zeros((rows, BLOCK), jnp.float32)
        total = jnp.zeros((rows, head), jnp.float32)
        start = 0
        for ref, length, bias in segments:
            weights = jnp.exp2(score_buf[:, start : start + length] - top)
            for n in range(length // BLOCK):
                mass = mass + weights[:, n * BLOCK : (n + 1) * BLOCK]
            total = total + jnp.dot(
                weights.astype(jnp.bfloat16), ref[1, h], preferred_element_type=jnp.float32
            )
            start += length
        result = total / jnp.sum(mass, axis=1, keepdims=True)
        heads_ref[pl.ds(first, rows), cols(h)] = result.astype(jnp.bfloat16)

    def ready(h):
        for which in range(3):
            load(h, which).wait()
        for which in range(2):
            wait_for(SIBLING, h, which)

        @pl.when(late == 0)
        def _():
            for which in range(2):
                far_send(h, which).wait_recv()

        for which in range(2):
            wait_for(RELAYED, h, which)

    def relay(h, which):
        wait_for(ACROSS, h, which)

        @pl.when(late == 1)
        def _():
            pass_on(ALONG, ACROSS, h, which, along_to).start()

        @pl.when(late == 0)
        def _():
            gather_forward(h, which)
            far_send(h, which).start()
            pass_on(RELAYED, ACROSS, h, which, sibling).start()

        gather_far(0, ACROSS, h, which, across_pick)

    def relay_late(h, which):
        wait_for(ALONG, h, which)
        pass_on(RELAYED, ALONG, h, which, sibling).start()
        gather_far(1, ALONG, h, which, along_pick)

    def got(rel, r):
        w_x(rel, r, g).start()
        w_s(rel, r, g).start()

    def z_arrives(k, rel):
        r = row_of(k)
        w_z(rel, r, 0).wait_recv()

        @pl.when(middle == 1)
        def _():
            w_z(rel, r, 0 if k == 1 else 1).start()

        got(rel, r)

    def twin_arrives(k, rel):
        r = row_of(k)
        w_x(rel, r, 1 - g).wait_recv()
        w_s(rel, r, 1 - g).start()

    def at(i, end, mid, core):
        return pl.when((i == jnp.where(middle == 1, mid, end)) & (c == core))

    def weight_step(i):
        @at(i, 0, 0, 0)
        def _():
            w_y_wait_row(z)
            w_z(1, z, 0).start()

            @pl.when(middle == 1)
            def _():
                w_z(1, z, 1).start()

            got(1, z)

        for core, k, end, mid in ((0, 1, 0, 0), (0, 2, 1, 0), (0, 3, 3, 2), (1, 1, 1, 1), (1, 2, 2, 1), (1, 3, 6, 5)):

            @at(i, end, mid, core)
            def _():
                z_arrives(k, 0)

        for core, k, end, mid in ((0, 1, 2, 2), (0, 2, 3, 2), (0, 3, 5, 4), (1, 1, 3, 3), (1, 2, 4, 3), (1, 3, 8, 7)):

            @at(i, end, mid, core)
            def _():
                twin_arrives(k, 0)

        for k, end, mid in ((1, 1, 1), (2, 2, 1), (3, 4, 3)):

            @at(i, end, mid, 0)
            def _():
                z_arrives(k, 1)

        for k, end, mid in ((0, 2, 2), (1, 3, 3), (2, 4, 3), (3, 6, 5)):

            @at(i, end, mid, 0)
            def _():
                twin_arrives(k, 1)

        for k, when in ((0, 8), (1, 10), (2, 11), (3, 11)):

            @at(i, when, when, 1)
            def _():
                for q in range(SLICES):
                    t_y(row_of(k), q, own=k == 0).start()

        for k, when in ((0, 10), (1, 12), (2, 13)):

            @at(i, when, when, 1)
            def _():
                across_arrives(k)

    def w_y_wait_row(r):
        place = w_place(r, 1 - y, c, g)
        w_copy(
            w_buf.at[place], w_place(r, 1 - y, c, g), (wy_send.at[r], wy_recv.at[r]), {"blk": across}
        ).wait_recv()

    def across_arrives(k):
        r = row_of(k)
        for q in range(SLICES):
            t_y_wait(r, q)
            t_x(r, g, q).start()
            t_s(r, g, q).start()

    def step(i, carry):
        def part_step(part, carry):
            @pl.when(i < HEADS)
            def _():
                relay(i, part)

            @pl.when((i >= LAG - 1) & (i < HEADS + LAG - 1) & (late == 1))
            def _():
                relay_late(i - LAG + 1, part)

            @pl.when((i >= LAG) & (part == 0))
            def _():
                ready(i - LAG)

            @pl.when(i >= LAG)
            def _():
                head_rows(i - LAG, part)

            return carry

        lax.fori_loop(0, 2, part_step, 0)

        @pl.when(i + LOOKAHEAD < HEADS)
        def _():
            begin_across(i + LOOKAHEAD, 0)

        weight_step(i)
        return carry

    lax.fori_loop(0, HEADS + LAG, step, 0)

    w_keep.wait()
    chunk = 4 * width
    for k in range(4):
        r = row_of(k)

        @pl.when(c == 1)
        def _():
            if k + 1 == 3:
                across_arrives(3)
            for q in range(SLICES):
                t_x(r, 1 - g, q).wait_recv()
                t_s(r, 1 - g, q).start()

        for rel in range(2):
            for part in range(2):

                @pl.when((c == 1) | (rel == 0))
                def _():
                    place = w_place(r, column(rel), 1 - c, part)
                    w_copy(
                        w_buf.at[place], place,
                        (ws_send.at[part, rel, r], ws_recv.at[part, rel, r]), {"blk": sibling},
                    ).wait_recv()

        @pl.when(c == 0)
        def _():
            for part in range(2):
                for q in range(SLICES):
                    t_s(r, part, q).wait_recv()

        def tile(t, carry):
            place = pl.ds(pl.multiple_of(r * 4 * width + t * chunk, 128), chunk)
            out_ref[:, place] = nt_dot(heads_ref[...], w_buf[place, :]).astype(out_ref.dtype)
            return carry

        lax.fori_loop(0, 4 * width // chunk, tile, 0)

    def finish(h, carry):
        for kind in (ACROSS, SIBLING, RELAYED):
            for which in range(2):
                own_send(kind, h, which, sibling).wait_send()

        @pl.when(late == 1)
        def _():
            for which in range(2):
                own_send(ALONG, h, which, sibling).wait_send()

        @pl.when(late == 0)
        def _():
            for which in range(2):
                far_send(h, which).wait_send()

        return carry

    lax.fori_loop(0, HEADS, finish, 0)

    def z_sent(rel):
        w_z(rel, z, 0).wait_send()

        @pl.when(middle == 1)
        def _():
            w_z(rel, z, 1).wait_send()
            w_z(rel, row_of(1), 0).wait_send()
            w_z(rel, row_of(2), 1).wait_send()
            w_z(rel, row_of(3), 1).wait_send()

    z_sent(0)

    @pl.when(c == 0)
    def _():
        z_sent(1)
        w_y(z).wait_send()

    for k in range(4):
        r = row_of(k)
        for rel in range(2):

            @pl.when((c == 0) | (rel == 0))
            def _():
                if k or rel:
                    w_x(rel, r, g).wait_send()
                for part in range(2):
                    w_s(rel, r, part).wait_send()

        @pl.when(c == 1)
        def _():
            for q in range(SLICES):
                t_y(r, q).wait_send()
                t_x(r, g, q).wait_send()
                for part in range(2):
                    t_s(r, part, q).wait_send()


def fused(queries, key_rows, value_rows, block_mask, weight):
    tok, feat = queries.shape
    head = feat // HEADS
    width = 16 * weight.shape[0]
    per_slab = tok // BLOCK
    columns = 3 * tok + 4 * BLOCK
    dma = pltpu.SemaphoreType.DMA
    bf16, f32 = jnp.bfloat16, jnp.float32
    scratch = [
        pltpu.VMEM((HEADS, tok, head), bf16),
        pltpu.VMEM((5, 2, HEADS, tok, head), bf16),
        pltpu.VMEM((2, 2, HEADS, 2 * BLOCK, head), bf16),
        pltpu.VMEM((2, HEADS, 2 * BLOCK, head), bf16),
        pltpu.VMEM((min(256, tok), columns), f32),
        pltpu.VMEM((tok, feat), bf16),
        pltpu.VMEM((width, feat), bf16),
        pltpu.SMEM(block_mask.shape, jnp.int32),
        pltpu.SMEM((per_slab, 2 * per_slab + 4), f32),
        pltpu.VMEM((2, 16, head), bf16),
        pltpu.VMEM((2, 16, head), bf16),
        dma((4, HEADS, 2)),
        dma((4, HEADS, 2)),
        dma((HEADS, 3)),
        dma((2,)),
        dma((2,)),
        dma((2, 4, 2)),
        dma((2, 4)),
        dma((4,)),
        dma((4,)),
        dma((2, 4)),
        dma((2, 4)),
        dma((2, 2, 4)),
        dma((2, 2, 4)),
        dma((4, SLICES)),
        dma((4, SLICES)),
        dma((4, SLICES)),
        dma((4, SLICES)),
        dma((2, 4, SLICES)),
        dma((2, 4, SLICES)),
    ]
    return pl.pallas_call(
        fused_kernel,
        out_shape=jax.ShapeDtypeStruct((tok, width), bf16),
        in_specs=[pl.BlockSpec(memory_space=pl.ANY)] * 5,
        out_specs=pl.BlockSpec(memory_space=pltpu.VMEM),
        scratch_shapes=scratch,
        compiler_params=pltpu.CompilerParams(
            collective_id=0, has_side_effects=True, vmem_limit_bytes=60 * 2**20
        ),
    )(queries, key_rows, value_rows, block_mask, weight)


def attend_kernel(slabs, q_hbm, k_hbm, v_hbm, bias_ref, heads_ref, q_buf, kv_buf, score_buf, send_sem, recv_sem, load_sem):
    tok, feat = q_hbm.shape
    head = feat // HEADS
    rows = min(256, tok)
    blocks = rows // BLOCK
    factor = math.log2(math.e) / math.sqrt(head)
    s = lax.axis_index("blk")
    c = lax.rem(s, 2)
    y = lax.rem(s // 2, 2)
    sibling = s + 1 - 2 * c
    across = s + 2 - 4 * y
    along_to = lax.rem(s + 4 - 8 * y + slabs, slabs)
    along_from = lax.rem(s - 4 + 8 * y + slabs, slabs)
    late = lax.rem(y + c, 2)

    def cols(h):
        return pl.ds(pl.multiple_of(h * head, head), head)

    def load(h, which):
        src = (k_hbm, v_hbm, q_hbm)[which]
        dst = q_buf.at[h] if which == 2 else kv_buf.at[OWN, which, h]
        return pltpu.make_async_copy(src.at[:, cols(h)], dst, load_sem.at[h, which])

    def send(kind, h, which, source, target):
        return pltpu.make_async_remote_copy(
            src_ref=source,
            dst_ref=kv_buf.at[kind, which, h],
            send_sem=send_sem.at[kind - 1, h, which],
            recv_sem=recv_sem.at[kind - 1, h, which],
            device_id={"blk": target},
            device_id_type=MESH,
        )

    def own_send(kind, h, which, target):
        return send(kind, h, which, (k_hbm, v_hbm)[which].at[:, cols(h)], target)

    def pass_on(kind, held, h, which, target):
        return send(kind, h, which, kv_buf.at[held, which, h], target)

    def wait_for(kind, h, which):
        own_send(kind, h, which, sibling).wait_recv()

    def arrived(kind, h):
        for which in range(2):
            wait_for(kind, h, which)

    barrier = pltpu.get_barrier_semaphore()
    peers = (sibling, across, along_to, along_from)
    for device in peers:
        pl.semaphore_signal(barrier, inc=1, device_id={"blk": device}, device_id_type=MESH)
    pl.semaphore_wait(barrier, len(peers))

    def begin_across(h, carry):
        for which in range(2):
            own_send(ACROSS, h, which, across).start()
        return carry

    def begin(h, carry):
        for which in range(2):
            own_send(SIBLING, h, which, sibling).start()
        for which in range(3):
            load(h, which).start()
        return carry

    lax.fori_loop(0, LOOKAHEAD, begin_across, 0)
    lax.fori_loop(0, HEADS, begin, 0)

    def head_rows(h, part):
        first = pl.multiple_of(part * rows, rows)
        q = q_buf[h, pl.ds(first, rows), :]
        peak = jnp.full((rows, 128), NEG, jnp.float32)
        for j in range(5):
            raw = nt_dot(q, kv_buf[j, 0, h]) * factor
            for b in range(blocks):
                for n in range(tok // BLOCK):
                    col = j * tok + n * BLOCK
                    piece = raw[b * BLOCK : (b + 1) * BLOCK, n * BLOCK : (n + 1) * BLOCK]
                    piece = piece + bias_ref[part * blocks + b, :, col : col + BLOCK]
                    score_buf[b * BLOCK : (b + 1) * BLOCK, col : col + BLOCK] = piece
            for n in range(tok // BLOCK):
                col = j * tok + n * BLOCK
                peak = jnp.maximum(peak, score_buf[:, col : col + BLOCK])
        top = jnp.max(peak, axis=1, keepdims=True)
        mass = jnp.zeros((rows, 128), jnp.float32)
        total = jnp.zeros((rows, head), jnp.float32)
        for j in range(5):
            weights = jnp.exp2(score_buf[:, j * tok : (j + 1) * tok] - top)
            for n in range(tok // BLOCK):
                mass = mass + weights[:, n * BLOCK : (n + 1) * BLOCK]
            total = total + jnp.dot(
                weights.astype(jnp.bfloat16), kv_buf[j, 1, h], preferred_element_type=jnp.float32
            )
        result = total / jnp.sum(mass, axis=1, keepdims=True)
        heads_ref[pl.ds(first, rows), cols(h)] = result.astype(jnp.bfloat16)

    def compute(h):
        for which in range(3):
            load(h, which).wait()
        arrived(SIBLING, h)

        @pl.when(late == 0)
        def _():
            arrived(ALONG, h)

        arrived(RELAYED, h)

        def part_step(part, carry):
            head_rows(h, part)
            return carry

        lax.fori_loop(0, tok // rows, part_step, 0)

    def relay_late(h):
        for which in range(2):
            wait_for(ALONG, h, which)
            pass_on(RELAYED, ALONG, h, which, sibling).start()

    def step(i, carry):
        @pl.when((i >= 2) & (i < HEADS))
        def _():
            compute(i - 2)

        @pl.when(i < HEADS)
        def _():
            for which in range(2):
                wait_for(ACROSS, i, which)
                pass_on(ALONG, ACROSS, i, which, along_to).start()

                @pl.when(late == 0)
                def _():
                    pass_on(RELAYED, ACROSS, i, which, sibling).start()

        @pl.when(i + LOOKAHEAD < HEADS)
        def _():
            begin_across(i + LOOKAHEAD, 0)

        @pl.when((i >= 1) & (i < HEADS + 1) & (late == 1))
        def _():
            relay_late(i - 1)

        @pl.when(i >= HEADS)
        def _():
            compute(i - 2)

        return carry

    lax.fori_loop(0, HEADS + 2, step, 0)

    def finish(h, carry):
        for kind in (ACROSS, ALONG, SIBLING, RELAYED):
            for which in range(2):
                own_send(kind, h, which, sibling).wait_send()
        return carry

    lax.fori_loop(0, HEADS, finish, 0)


def attend(slabs, queries, key_rows, value_rows, bias):
    tok, feat = queries.shape
    head = feat // HEADS
    return pl.pallas_call(
        functools.partial(attend_kernel, slabs),
        out_shape=jax.ShapeDtypeStruct((tok, feat), jnp.bfloat16),
        in_specs=[pl.BlockSpec(memory_space=pl.ANY)] * 3 + [pl.BlockSpec(memory_space=pltpu.VMEM)],
        out_specs=pl.BlockSpec(memory_space=pltpu.VMEM),
        scratch_shapes=[
            pltpu.VMEM((HEADS, tok, head), jnp.bfloat16),
            pltpu.VMEM((5, 2, HEADS, tok, head), jnp.bfloat16),
            pltpu.VMEM((min(256, tok), 5 * tok), jnp.float32),
            pltpu.SemaphoreType.DMA((4, HEADS, 2)),
            pltpu.SemaphoreType.DMA((4, HEADS, 2)),
            pltpu.SemaphoreType.DMA((HEADS, 3)),
        ],
        compiler_params=pltpu.CompilerParams(
            collective_id=0, has_side_effects=True, vmem_limit_bytes=60 * 2**20
        ),
    )(queries, key_rows, value_rows, bias)


def local(slabs, groups, queries, key_rows, value_rows, block_mask, out_weight):
    per_slab = queries.shape[0] // BLOCK
    if groups == 2 and slabs == 16 and per_slab == 4 and out_weight.shape[1] % 64 == 0:
        return fused(queries, key_rows, value_rows, block_mask, out_weight.T)
    s = lax.axis_index("blk")
    c = s % 2
    y = (s // 2) % 2
    table = jnp.where(block_mask > 0, 0.0, NEG).astype(jnp.float32)
    table = table.reshape(block_mask.shape[0], 2 * RADIUS + 1, per_slab)
    back2, back1, own, next1, next2 = (table[:, d] for d in range(5))
    ordered = jnp.concatenate(
        (
            own,
            jnp.where(y == 0, next2, back2),
            jnp.where(y == 0, back2, next2),
            jnp.where(c == 0, next1, back1),
            jnp.where(c == 0, back1, next1),
        ),
        axis=1,
    )
    bias = jnp.repeat(ordered, BLOCK, axis=1)[:, None, :]
    attention = attend(slabs, queries, key_rows, value_rows, bias)
    weight = lax.all_gather(out_weight, "blk", axis=1, tiled=True)
    return jnp.dot(attention, weight, preferred_element_type=jnp.float32).astype(jnp.bfloat16)


def solution(mesh):
    in_specs = (
        P(("groups", "blk"), None),
        P(("groups", "blk"), None),
        P(("groups", "blk"), None),
        P("blk", None),
        P(None, "blk"),
    )
    out_specs = P(("groups", "blk"), None)
    body = functools.partial(local, mesh.shape["blk"], mesh.shape["groups"])
    return jax.shard_map(body, mesh=mesh, in_specs=in_specs, out_specs=out_specs, check_vma=False)
```

```python
import functools
import math

import jax
import jax.numpy as jnp
from jax import lax
from jax.experimental import pallas as pl
from jax.experimental.pallas import tpu as pltpu
from jax.sharding import PartitionSpec as P

HEADS = 12
BLOCK = 128
RADIUS = 2
NEG = -1e30
OWN, ACROSS, ALONG, SIBLING, RELAYED = range(5)
MESH = pl.DeviceIdType.MESH


def nt_dot(a, b):
    return lax.dot_general(a, b, (((1,), (1,)), ((), ())), preferred_element_type=jnp.float32)


LOOKAHEAD = 4
LAG = 3
SLICES = 3

def fused_kernel(
    q_hbm, k_hbm, v_hbm, mask_hbm, w_hbm, out_ref,
    q_buf, kv_buf, far_buf, fwd_buf, score_buf, heads_ref, w_buf, mask_buf, bias_buf, note_out, note_in,
    send_sem, recv_sem, load_sem, small_sem, note_sem,
    wz_send, wz_recv, wy_send, wy_recv, wx_send, wx_recv, ws_send, ws_recv,
    ty_send, ty_recv, tx_send, tx_recv, ts_send, ts_recv,
):
    tok, feat = q_hbm.shape
    head = feat // HEADS
    rows = min(256, tok)
    blocks = rows // BLOCK
    per_slab = tok // BLOCK
    factor = math.log2(math.e) / math.sqrt(head)
    slabs = 16
    s = lax.axis_index("blk")
    g = lax.axis_index("groups")
    c = lax.rem(s, 2)
    y = lax.rem(s // 2, 2)
    z = s // 4
    sibling = s + 1 - 2 * c
    across = s + 2 - 4 * y
    along_to = lax.rem(s + 4 - 8 * y + slabs, slabs)
    along_from = lax.rem(s - 4 + 8 * y + slabs, slabs)
    late = lax.rem(y + c, 2)
    inward = jnp.where(z < 2, 1, -1)
    middle = jnp.where((z == 1) | (z == 2), 1, 0)
    inner = s + 4 * inward
    outer = s - 4 * inward

    def row_of(k):
        back = 0 if k == 0 else 2 if k == 1 else 1
        return z + inward * (k - middle * back)

    def cols(h):
        return pl.ds(pl.multiple_of(h * head, head), head)

    def load(h, which):
        src = (k_hbm, v_hbm, q_hbm)[which]
        dst = q_buf.at[h] if which == 2 else kv_buf.at[OWN, which, h]
        return pltpu.make_async_copy(src.at[:, cols(h)], dst, load_sem.at[h, which])

    def send(kind, h, which, source, place, target):
        return pltpu.make_async_remote_copy(
            src_ref=source,
            dst_ref=place,
            send_sem=send_sem.at[kind - 1, h, which],
            recv_sem=recv_sem.at[kind - 1, h, which],
            device_id={"blk": target},
            device_id_type=MESH,
        )

    def own_send(kind, h, which, target):
        return send(kind, h, which, (k_hbm, v_hbm)[which].at[:, cols(h)], kv_buf.at[kind, which, h], target)

    def pass_on(kind, held, h, which, target):
        return send(kind, h, which, kv_buf.at[held, which, h], kv_buf.at[kind, which, h], target)

    def far_send(h, which):
        return send(ALONG, h, which, fwd_buf.at[which, h], far_buf.at[1, which, h], along_to)

    def wait_for(kind, h, which):
        pass_on(kind, kind, h, which, sibling).wait_recv()

    width = w_hbm.shape[0]
    half = width // 2

    def w_place(r, col, core, part):
        index = 4 * r + 2 * col + core
        return pl.ds(pl.multiple_of(index * width + part * half, 32), half)

    def w_copy(source, place, sems, device):
        return pltpu.make_async_remote_copy(
            src_ref=source,
            dst_ref=w_buf.at[place],
            send_sem=sems[0],
            recv_sem=sems[1],
            device_id=device,
            device_id_type=MESH,
        )

    own_half = w_hbm.at[pl.ds(pl.multiple_of(g * half, 32), half)]

    def column(rel):
        return y if rel == 0 else 1 - y

    def w_z(rel, r, way, own=False):
        place = w_place(r, column(rel), c, g)
        return w_copy(
            own_half if own else w_buf.at[place], place,
            (wz_send.at[rel, r, way], wz_recv.at[rel, r]),
            {"blk": outer if way else inner},
        )

    def w_y(r, own=False):
        place = w_place(r, y, c, g)
        return w_copy(
            own_half if own else w_buf.at[place], place,
            (wy_send.at[r], wy_recv.at[r]), {"blk": across},
        )

    thin = half // SLICES

    def slice_rows(start, q):
        return pl.ds(pl.multiple_of(start + q * thin, 32), thin)

    def slice_place(r, col, part, q):
        return slice_rows((4 * r + 2 * col + 1) * width + part * half, q)

    def t_y(r, q, own=False):
        place = slice_place(r, y, g, q)
        return w_copy(
            w_hbm.at[slice_rows(g * half, q)] if own else w_buf.at[place], place,
            (ty_send.at[r, q], ty_recv.at[r, q]), {"blk": across},
        )

    def t_y_wait(r, q):
        place = slice_place(r, 1 - y, g, q)
        w_copy(w_buf.at[place], place, (ty_send.at[r, q], ty_recv.at[r, q]), {"blk": across}).wait_recv()

    def t_x(r, part, q):
        place = slice_place(r, 1 - y, part, q)
        return w_copy(w_buf.at[place], place, (tx_send.at[r, q], tx_recv.at[r, q]), {"groups": 1 - g})

    def t_s(r, part, q):
        place = slice_place(r, 1 - y, part, q)
        return w_copy(
            w_buf.at[place], place, (ts_send.at[part, r, q], ts_recv.at[part, r, q]), {"blk": sibling}
        )

    def w_x(rel, r, part):
        place = w_place(r, column(rel), c, part)
        return w_copy(
            w_buf.at[place], place, (wx_send.at[rel, r], wx_recv.at[rel, r]), {"groups": 1 - g}
        )

    def w_s(rel, r, part, own=False):
        place = w_place(r, column(rel), c, part)
        source = w_hbm.at[pl.ds(pl.multiple_of(part * half, 32), half)] if own else w_buf.at[place]
        return w_copy(
            source, place, (ws_send.at[part, rel, r], ws_recv.at[part, rel, r]), {"blk": sibling}
        )

    own_place = pl.ds(pl.multiple_of(s * width, 32), width)
    w_keep = pltpu.make_async_copy(w_hbm, w_buf.at[own_place], small_sem.at[1])
    mask_load = pltpu.make_async_copy(mask_hbm, mask_buf, small_sem.at[0])
    note = pltpu.make_async_remote_copy(
        src_ref=note_out,
        dst_ref=note_in,
        send_sem=note_sem.at[0],
        recv_sem=note_sem.at[1],
        device_id={"blk": along_from},
        device_id_type=MESH,
    )

    mask_load.start()
    barrier = pltpu.get_barrier_semaphore()
    peers = [{"blk": device} for device in (sibling, across, along_to, along_from)]
    peers.append({"groups": 1 - g})
    for device in peers:
        pl.semaphore_signal(barrier, inc=1, device_id=device, device_id_type=MESH)
    pl.semaphore_wait(barrier, len(peers))

    def begin_across(h, carry):
        for which in range(2):
            own_send(ACROSS, h, which, across).start()
        return carry

    def begin(h, carry):
        for which in range(2):
            own_send(SIBLING, h, which, sibling).start()
        for which in range(3):
            load(h, which).start()
        return carry

    begin_across(0, 0)
    w_z(0, z, 0, own=True).start()

    @pl.when(middle == 1)
    def _():
        w_z(0, z, 1, own=True).start()

    begin_across(1, 0)

    @pl.when(c == 0)
    def _():
        w_y(z, own=True).start()

    lax.fori_loop(2, LOOKAHEAD, begin_across, 0)
    lax.fori_loop(0, HEADS, begin, 0)
    w_keep.start()
    for part in range(2):
        w_s(0, z, part, own=True).start()

    mask_load.wait()
    base_across = jnp.where(y == 0, 4 * per_slab, 0)
    base_along = 4 * per_slab - base_across
    base_sibling = jnp.where(c == 0, 3 * per_slab, per_slab)
    base_relayed = 4 * per_slab - base_sibling

    def admitted(base):
        used = []
        for n in range(per_slab):
            value = mask_buf[0, base + n]
            for b in range(1, per_slab):
                value = jnp.maximum(value, mask_buf[b, base + n])
            used.append(value > 0)
        first = jnp.where(used[0], 0, jnp.where(used[1], 1, 2))
        second = jnp.where(used[3], 3, jnp.where(used[2], 2, 1))
        return first, second

    across_pick = admitted(base_across)
    along_pick = admitted(base_along)
    for n in range(2):
        level = jnp.full(note_out.shape[1:], along_pick[n].astype(jnp.float32), jnp.float32)
        note_out[n] = level.astype(jnp.bfloat16)
    note.start()

    def offset(value):
        return jnp.where(value > 0, 0.0, NEG).astype(jnp.float32)

    for b in range(per_slab):
        for n in range(per_slab):
            bias_buf[b, n] = offset(mask_buf[b, base_sibling + n])
            bias_buf[b, per_slab + n] = offset(mask_buf[b, base_relayed + n])
        for n in range(2):
            bias_buf[b, 2 * per_slab + n] = offset(mask_buf[b, base_across + across_pick[n]])
            bias_buf[b, 2 * per_slab + 2 + n] = offset(mask_buf[b, base_along + along_pick[n]])
    note.wait()

    def gather_far(kind, held, h, which, picks):
        piece = [kv_buf[held, which, h, n * BLOCK : (n + 1) * BLOCK, :] for n in range(per_slab)]
        first = lax.select(picks[0] == 0, piece[0], lax.select(picks[0] == 1, piece[1], piece[2]))
        second = lax.select(picks[1] == 3, piece[3], lax.select(picks[1] == 2, piece[2], piece[1]))
        far_buf[kind, which, h, :BLOCK, :] = first
        far_buf[kind, which, h, BLOCK:, :] = second

    def gather_forward(h, which):
        size = note_in.shape[1]
        first, second = note_in[0], note_in[1]
        for t in range(BLOCK // size):
            piece = [
                kv_buf[ACROSS, which, h, n * BLOCK + t * size : n * BLOCK + (t + 1) * size, :]
                for n in range(per_slab)
            ]
            fwd_buf[which, h, t * size : (t + 1) * size, :] = jnp.where(
                first == 0, piece[0], jnp.where(first == 1, piece[1], piece[2])
            )
            fwd_buf[which, h, BLOCK + t * size : BLOCK + (t + 1) * size, :] = jnp.where(
                second == 3, piece[3], jnp.where(second == 2, piece[2], piece[1])
            )

    def head_rows(h, part):
        first = pl.multiple_of(part * rows, rows)
        q = q_buf[h, pl.ds(first, rows), :]
        segments = [
            (kv_buf.at[OWN], tok, None),
            (kv_buf.at[SIBLING], tok, 0),
            (kv_buf.at[RELAYED], tok, per_slab),
            (far_buf.at[0], 2 * BLOCK, 2 * per_slab),
            (far_buf.at[1], 2 * BLOCK, 2 * per_slab + 2),
        ]
        peak = jnp.full((rows, BLOCK), NEG, jnp.float32)
        start = 0
        for ref, length, bias in segments:
            raw = nt_dot(q, ref[0, h]) * factor
            for n in range(length // BLOCK):
                col = start + n * BLOCK
                for b in range(blocks):
                    piece = raw[b * BLOCK : (b + 1) * BLOCK, n * BLOCK : (n + 1) * BLOCK]
                    if bias is not None:
                        piece = piece + bias_buf[part * blocks + b, bias + n]
                    score_buf[b * BLOCK : (b + 1) * BLOCK, col : col + BLOCK] = piece
                peak = jnp.maximum(peak, score_buf[:, col : col + BLOCK])
            start += length
        top = jnp.max(peak, axis=1, keepdims=True)
        mass = jnp.zeros((rows, BLOCK), jnp.float32)
        total = jnp.zeros((rows, head), jnp.float32)
        start = 0
        for ref, length, bias in segments:
            weights = jnp.exp2(score_buf[:, start : start + length] - top)
            for n in range(length // BLOCK):
                mass = mass + weights[:, n * BLOCK : (n + 1) * BLOCK]
            total = total + jnp.dot(
                weights.astype(jnp.bfloat16), ref[1, h], preferred_element_type=jnp.float32
            )
            start += length
        result = total / jnp.sum(mass, axis=1, keepdims=True)
        heads_ref[pl.ds(first, rows), cols(h)] = result.astype(jnp.bfloat16)

    def ready(h):
        for which in range(3):
            load(h, which).wait()
        for which in range(2):
            wait_for(SIBLING, h, which)

        @pl.when(late == 0)
        def _():
            for which in range(2):
                far_send(h, which).wait_recv()

        for which in range(2):
            wait_for(RELAYED, h, which)

    def relay(h, which):
        wait_for(ACROSS, h, which)

        @pl.when(late == 1)
        def _():
            pass_on(ALONG, ACROSS, h, which, along_to).start()

        @pl.when(late == 0)
        def _():
            gather_forward(h, which)
            far_send(h, which).start()
            pass_on(RELAYED, ACROSS, h, which, sibling).start()

        gather_far(0, ACROSS, h, which, across_pick)

    def relay_late(h, which):
        wait_for(ALONG, h, which)
        pass_on(RELAYED, ALONG, h, which, sibling).start()
        gather_far(1, ALONG, h, which, along_pick)

    def got(rel, r):
        w_x(rel, r, g).start()
        w_s(rel, r, g).start()

    def z_arrives(k, rel):
        r = row_of(k)
        w_z(rel, r, 0).wait_recv()

        @pl.when(middle == 1)
        def _():
            w_z(rel, r, 0 if k == 1 else 1).start()

        got(rel, r)

    def twin_arrives(k, rel):
        r = row_of(k)
        w_x(rel, r, 1 - g).wait_recv()
        w_s(rel, r, 1 - g).start()

    def at(i, end, mid, core):
        return pl.when((i == jnp.where(middle == 1, mid, end)) & (c == core))

    def weight_step(i):
        @at(i, 0, 0, 0)
        def _():
            w_y_wait_row(z)
            w_z(1, z, 0).start()

            @pl.when(middle == 1)
            def _():
                w_z(1, z, 1).start()

            got(1, z)

        for core, k, end, mid in ((0, 1, 0, 0), (0, 2, 1, 0), (0, 3, 3, 2), (1, 1, 1, 1), (1, 2, 2, 1), (1, 3, 6, 5)):

            @at(i, end, mid, core)
            def _():
                z_arrives(k, 0)

        for core, k, end, mid in ((0, 1, 2, 2), (0, 2, 3, 2), (0, 3, 5, 4), (1, 1, 3, 3), (1, 2, 4, 3), (1, 3, 8, 7)):

            @at(i, end, mid, core)
            def _():
                twin_arrives(k, 0)

        for k, end, mid in ((1, 1, 1), (2, 2, 1), (3, 4, 3)):

            @at(i, end, mid, 0)
            def _():
                z_arrives(k, 1)

        for k, end, mid in ((0, 2, 2), (1, 3, 3), (2, 4, 3), (3, 6, 5)):

            @at(i, end, mid, 0)
            def _():
                twin_arrives(k, 1)

        for k, when in ((0, 4), (1, 10), (2, 11), (3, 11)):

            @at(i, when, when, 1)
            def _():
                for q in range(SLICES):
                    t_y(row_of(k), q, own=k == 0).start()

        for k, when in ((0, 6), (1, 12), (2, 13)):

            @at(i, when, when, 1)
            def _():
                across_arrives(k)

    def w_y_wait_row(r):
        place = w_place(r, 1 - y, c, g)
        w_copy(
            w_buf.at[place], w_place(r, 1 - y, c, g), (wy_send.at[r], wy_recv.at[r]), {"blk": across}
        ).wait_recv()

    def across_arrives(k):
        r = row_of(k)
        for q in range(SLICES):
            t_y_wait(r, q)
            t_x(r, g, q).start()
            t_s(r, g, q).start()

    def step(i, carry):
        def part_step(part, carry):
            @pl.when(i < HEADS)
            def _():
                relay(i, part)

            @pl.when((i >= LAG - 1) & (i < HEADS + LAG - 1) & (late == 1))
            def _():
                relay_late(i - LAG + 1, part)

            @pl.when((i >= LAG) & (part == 0))
            def _():
                ready(i - LAG)

            @pl.when(i >= LAG)
            def _():
                head_rows(i - LAG, part)

            return carry

        lax.fori_loop(0, 2, part_step, 0)

        @pl.when(i + LOOKAHEAD < HEADS)
        def _():
            begin_across(i + LOOKAHEAD, 0)

        weight_step(i)
        return carry

    lax.fori_loop(0, HEADS + LAG, step, 0)

    w_keep.wait()
    chunk = 4 * width
    for k in range(4):
        r = row_of(k)

        @pl.when(c == 1)
        def _():
            if k + 1 == 3:
                across_arrives(3)
            for q in range(SLICES):
                t_x(r, 1 - g, q).wait_recv()
                t_s(r, 1 - g, q).start()

        for rel in range(2):
            for part in range(2):

                @pl.when((c == 1) | (rel == 0))
                def _():
                    place = w_place(r, column(rel), 1 - c, part)
                    w_copy(
                        w_buf.at[place], place,
                        (ws_send.at[part, rel, r], ws_recv.at[part, rel, r]), {"blk": sibling},
                    ).wait_recv()

        @pl.when(c == 0)
        def _():
            for part in range(2):
                for q in range(SLICES):
                    t_s(r, part, q).wait_recv()

        def tile(t, carry):
            place = pl.ds(pl.multiple_of(r * 4 * width + t * chunk, 128), chunk)
            out_ref[:, place] = nt_dot(heads_ref[...], w_buf[place, :]).astype(out_ref.dtype)
            return carry

        lax.fori_loop(0, 4 * width // chunk, tile, 0)

    def finish(h, carry):
        for kind in (ACROSS, SIBLING, RELAYED):
            for which in range(2):
                own_send(kind, h, which, sibling).wait_send()

        @pl.when(late == 1)
        def _():
            for which in range(2):
                own_send(ALONG, h, which, sibling).wait_send()

        @pl.when(late == 0)
        def _():
            for which in range(2):
                far_send(h, which).wait_send()

        return carry

    lax.fori_loop(0, HEADS, finish, 0)

    def z_sent(rel):
        w_z(rel, z, 0).wait_send()

        @pl.when(middle == 1)
        def _():
            w_z(rel, z, 1).wait_send()
            w_z(rel, row_of(1), 0).wait_send()
            w_z(rel, row_of(2), 1).wait_send()
            w_z(rel, row_of(3), 1).wait_send()

    z_sent(0)

    @pl.when(c == 0)
    def _():
        z_sent(1)
        w_y(z).wait_send()

    for k in range(4):
        r = row_of(k)
        for rel in range(2):

            @pl.when((c == 0) | (rel == 0))
            def _():
                if k or rel:
                    w_x(rel, r, g).wait_send()
                for part in range(2):
                    w_s(rel, r, part).wait_send()

        @pl.when(c == 1)
        def _():
            for q in range(SLICES):
                t_y(r, q).wait_send()
                t_x(r, g, q).wait_send()
                for part in range(2):
                    t_s(r, part, q).wait_send()


def fused(queries, key_rows, value_rows, block_mask, weight):
    tok, feat = queries.shape
    head = feat // HEADS
    width = 16 * weight.shape[0]
    per_slab = tok // BLOCK
    columns = 3 * tok + 4 * BLOCK
    dma = pltpu.SemaphoreType.DMA
    bf16, f32 = jnp.bfloat16, jnp.float32
    scratch = [
        pltpu.VMEM((HEADS, tok, head), bf16),
        pltpu.VMEM((5, 2, HEADS, tok, head), bf16),
        pltpu.VMEM((2, 2, HEADS, 2 * BLOCK, head), bf16),
        pltpu.VMEM((2, HEADS, 2 * BLOCK, head), bf16),
        pltpu.VMEM((min(256, tok), columns), f32),
        pltpu.VMEM((tok, feat), bf16),
        pltpu.VMEM((width, feat), bf16),
        pltpu.SMEM(block_mask.shape, jnp.int32),
        pltpu.SMEM((per_slab, 2 * per_slab + 4), f32),
        pltpu.VMEM((2, 16, head), bf16),
        pltpu.VMEM((2, 16, head), bf16),
        dma((4, HEADS, 2)),
        dma((4, HEADS, 2)),
        dma((HEADS, 3)),
        dma((2,)),
        dma((2,)),
        dma((2, 4, 2)),
        dma((2, 4)),
        dma((4,)),
        dma((4,)),
        dma((2, 4)),
        dma((2, 4)),
        dma((2, 2, 4)),
        dma((2, 2, 4)),
        dma((4, SLICES)),
        dma((4, SLICES)),
        dma((4, SLICES)),
        dma((4, SLICES)),
        dma((2, 4, SLICES)),
        dma((2, 4, SLICES)),
    ]
    return pl.pallas_call(
        fused_kernel,
        out_shape=jax.ShapeDtypeStruct((tok, width), bf16),
        in_specs=[pl.BlockSpec(memory_space=pl.ANY)] * 5,
        out_specs=pl.BlockSpec(memory_space=pltpu.VMEM),
        scratch_shapes=scratch,
        compiler_params=pltpu.CompilerParams(
            collective_id=0, has_side_effects=True, vmem_limit_bytes=60 * 2**20
        ),
    )(queries, key_rows, value_rows, block_mask, weight)


def attend_kernel(slabs, q_hbm, k_hbm, v_hbm, bias_ref, heads_ref, q_buf, kv_buf, score_buf, send_sem, recv_sem, load_sem):
    tok, feat = q_hbm.shape
    head = feat // HEADS
    rows = min(256, tok)
    blocks = rows // BLOCK
    factor = math.log2(math.e) / math.sqrt(head)
    s = lax.axis_index("blk")
    c = lax.rem(s, 2)
    y = lax.rem(s // 2, 2)
    sibling = s + 1 - 2 * c
    across = s + 2 - 4 * y
    along_to = lax.rem(s + 4 - 8 * y + slabs, slabs)
    along_from = lax.rem(s - 4 + 8 * y + slabs, slabs)
    late = lax.rem(y + c, 2)

    def cols(h):
        return pl.ds(pl.multiple_of(h * head, head), head)

    def load(h, which):
        src = (k_hbm, v_hbm, q_hbm)[which]
        dst = q_buf.at[h] if which == 2 else kv_buf.at[OWN, which, h]
        return pltpu.make_async_copy(src.at[:, cols(h)], dst, load_sem.at[h, which])

    def send(kind, h, which, source, target):
        return pltpu.make_async_remote_copy(
            src_ref=source,
            dst_ref=kv_buf.at[kind, which, h],
            send_sem=send_sem.at[kind - 1, h, which],
            recv_sem=recv_sem.at[kind - 1, h, which],
            device_id={"blk": target},
            device_id_type=MESH,
        )

    def own_send(kind, h, which, target):
        return send(kind, h, which, (k_hbm, v_hbm)[which].at[:, cols(h)], target)

    def pass_on(kind, held, h, which, target):
        return send(kind, h, which, kv_buf.at[held, which, h], target)

    def wait_for(kind, h, which):
        own_send(kind, h, which, sibling).wait_recv()

    def arrived(kind, h):
        for which in range(2):
            wait_for(kind, h, which)

    barrier = pltpu.get_barrier_semaphore()
    peers = (sibling, across, along_to, along_from)
    for device in peers:
        pl.semaphore_signal(barrier, inc=1, device_id={"blk": device}, device_id_type=MESH)
    pl.semaphore_wait(barrier, len(peers))

    def begin_across(h, carry):
        for which in range(2):
            own_send(ACROSS, h, which, across).start()
        return carry

    def begin(h, carry):
        for which in range(2):
            own_send(SIBLING, h, which, sibling).start()
        for which in range(3):
            load(h, which).start()
        return carry

    lax.fori_loop(0, LOOKAHEAD, begin_across, 0)
    lax.fori_loop(0, HEADS, begin, 0)

    def head_rows(h, part):
        first = pl.multiple_of(part * rows, rows)
        q = q_buf[h, pl.ds(first, rows), :]
        peak = jnp.full((rows, 128), NEG, jnp.float32)
        for j in range(5):
            raw = nt_dot(q, kv_buf[j, 0, h]) * factor
            for b in range(blocks):
                for n in range(tok // BLOCK):
                    col = j * tok + n * BLOCK
                    piece = raw[b * BLOCK : (b + 1) * BLOCK, n * BLOCK : (n + 1) * BLOCK]
                    piece = piece + bias_ref[part * blocks + b, :, col : col + BLOCK]
                    score_buf[b * BLOCK : (b + 1) * BLOCK, col : col + BLOCK] = piece
            for n in range(tok // BLOCK):
                col = j * tok + n * BLOCK
                peak = jnp.maximum(peak, score_buf[:, col : col + BLOCK])
        top = jnp.max(peak, axis=1, keepdims=True)
        mass = jnp.zeros((rows, 128), jnp.float32)
        total = jnp.zeros((rows, head), jnp.float32)
        for j in range(5):
            weights = jnp.exp2(score_buf[:, j * tok : (j + 1) * tok] - top)
            for n in range(tok // BLOCK):
                mass = mass + weights[:, n * BLOCK : (n + 1) * BLOCK]
            total = total + jnp.dot(
                weights.astype(jnp.bfloat16), kv_buf[j, 1, h], preferred_element_type=jnp.float32
            )
        result = total / jnp.sum(mass, axis=1, keepdims=True)
        heads_ref[pl.ds(first, rows), cols(h)] = result.astype(jnp.bfloat16)

    def compute(h):
        for which in range(3):
            load(h, which).wait()
        arrived(SIBLING, h)

        @pl.when(late == 0)
        def _():
            arrived(ALONG, h)

        arrived(RELAYED, h)

        def part_step(part, carry):
            head_rows(h, part)
            return carry

        lax.fori_loop(0, tok // rows, part_step, 0)

    def relay_late(h):
        for which in range(2):
            wait_for(ALONG, h, which)
            pass_on(RELAYED, ALONG, h, which, sibling).start()

    def step(i, carry):
        @pl.when((i >= 2) & (i < HEADS))
        def _():
            compute(i - 2)

        @pl.when(i < HEADS)
        def _():
            for which in range(2):
                wait_for(ACROSS, i, which)
                pass_on(ALONG, ACROSS, i, which, along_to).start()

                @pl.when(late == 0)
                def _():
                    pass_on(RELAYED, ACROSS, i, which, sibling).start()

        @pl.when(i + LOOKAHEAD < HEADS)
        def _():
            begin_across(i + LOOKAHEAD, 0)

        @pl.when((i >= 1) & (i < HEADS + 1) & (late == 1))
        def _():
            relay_late(i - 1)

        @pl.when(i >= HEADS)
        def _():
            compute(i - 2)

        return carry

    lax.fori_loop(0, HEADS + 2, step, 0)

    def finish(h, carry):
        for kind in (ACROSS, ALONG, SIBLING, RELAYED):
            for which in range(2):
                own_send(kind, h, which, sibling).wait_send()
        return carry

    lax.fori_loop(0, HEADS, finish, 0)


def attend(slabs, queries, key_rows, value_rows, bias):
    tok, feat = queries.shape
    head = feat // HEADS
    return pl.pallas_call(
        functools.partial(attend_kernel, slabs),
        out_shape=jax.ShapeDtypeStruct((tok, feat), jnp.bfloat16),
        in_specs=[pl.BlockSpec(memory_space=pl.ANY)] * 3 + [pl.BlockSpec(memory_space=pltpu.VMEM)],
        out_specs=pl.BlockSpec(memory_space=pltpu.VMEM),
        scratch_shapes=[
            pltpu.VMEM((HEADS, tok, head), jnp.bfloat16),
            pltpu.VMEM((5, 2, HEADS, tok, head), jnp.bfloat16),
            pltpu.VMEM((min(256, tok), 5 * tok), jnp.float32),
            pltpu.SemaphoreType.DMA((4, HEADS, 2)),
            pltpu.SemaphoreType.DMA((4, HEADS, 2)),
            pltpu.SemaphoreType.DMA((HEADS, 3)),
        ],
        compiler_params=pltpu.CompilerParams(
            collective_id=0, has_side_effects=True, vmem_limit_bytes=60 * 2**20
        ),
    )(queries, key_rows, value_rows, bias)


def local(slabs, groups, queries, key_rows, value_rows, block_mask, out_weight):
    per_slab = queries.shape[0] // BLOCK
    if groups == 2 and slabs == 16 and per_slab == 4 and out_weight.shape[1] % 64 == 0:
        return fused(queries, key_rows, value_rows, block_mask, out_weight.T)
    s = lax.axis_index("blk")
    c = s % 2
    y = (s // 2) % 2
    table = jnp.where(block_mask > 0, 0.0, NEG).astype(jnp.float32)
    table = table.reshape(block_mask.shape[0], 2 * RADIUS + 1, per_slab)
    back2, back1, own, next1, next2 = (table[:, d] for d in range(5))
    ordered = jnp.concatenate(
        (
            own,
            jnp.where(y == 0, next2, back2),
            jnp.where(y == 0, back2, next2),
            jnp.where(c == 0, next1, back1),
            jnp.where(c == 0, back1, next1),
        ),
        axis=1,
    )
    bias = jnp.repeat(ordered, BLOCK, axis=1)[:, None, :]
    attention = attend(slabs, queries, key_rows, value_rows, bias)
    weight = lax.all_gather(out_weight, "blk", axis=1, tiled=True)
    return jnp.dot(attention, weight, preferred_element_type=jnp.float32).astype(jnp.bfloat16)


def solution(mesh):
    in_specs = (
        P(("groups", "blk"), None),
        P(("groups", "blk"), None),
        P(("groups", "blk"), None),
        P("blk", None),
        P(None, "blk"),
    )
    out_specs = P(("groups", "blk"), None)
    body = functools.partial(local, mesh.shape["blk"], mesh.shape["groups"])
    return jax.shard_map(body, mesh=mesh, in_specs=in_specs, out_specs=out_specs, check_vma=False)
```

```python
import functools
import math

import jax
import jax.numpy as jnp
from jax import lax
from jax.experimental import pallas as pl
from jax.experimental.pallas import tpu as pltpu
from jax.sharding import PartitionSpec as P

HEADS = 12
BLOCK = 128
RADIUS = 2
NEG = -1e30
OWN, ACROSS, ALONG, SIBLING, RELAYED = range(5)
MESH = pl.DeviceIdType.MESH


def nt_dot(a, b):
    return lax.dot_general(a, b, (((1,), (1,)), ((), ())), preferred_element_type=jnp.float32)


LOOKAHEAD = 4
LAG = 3
SLICES = 1

def fused_kernel(
    q_hbm, k_hbm, v_hbm, mask_hbm, w_hbm, out_ref,
    q_buf, kv_buf, far_buf, fwd_buf, score_buf, heads_ref, w_buf, mask_buf, bias_buf, note_out, note_in,
    send_sem, recv_sem, load_sem, small_sem, note_sem,
    wz_send, wz_recv, wy_send, wy_recv, wx_send, wx_recv, ws_send, ws_recv,
    ty_send, ty_recv, tx_send, tx_recv, ts_send, ts_recv,
):
    tok, feat = q_hbm.shape
    head = feat // HEADS
    rows = min(256, tok)
    blocks = rows // BLOCK
    per_slab = tok // BLOCK
    factor = math.log2(math.e) / math.sqrt(head)
    slabs = 16
    s = lax.axis_index("blk")
    g = lax.axis_index("groups")
    c = lax.rem(s, 2)
    y = lax.rem(s // 2, 2)
    z = s // 4
    sibling = s + 1 - 2 * c
    across = s + 2 - 4 * y
    along_to = lax.rem(s + 4 - 8 * y + slabs, slabs)
    along_from = lax.rem(s - 4 + 8 * y + slabs, slabs)
    late = lax.rem(y + c, 2)
    inward = jnp.where(z < 2, 1, -1)
    middle = jnp.where((z == 1) | (z == 2), 1, 0)
    inner = s + 4 * inward
    outer = s - 4 * inward

    def row_of(k):
        back = 0 if k == 0 else 2 if k == 1 else 1
        return z + inward * (k - middle * back)

    def cols(h):
        return pl.ds(pl.multiple_of(h * head, head), head)

    def load(h, which):
        src = (k_hbm, v_hbm, q_hbm)[which]
        dst = q_buf.at[h] if which == 2 else kv_buf.at[OWN, which, h]
        return pltpu.make_async_copy(src.at[:, cols(h)], dst, load_sem.at[h, which])

    def send(kind, h, which, source, place, target):
        return pltpu.make_async_remote_copy(
            src_ref=source,
            dst_ref=place,
            send_sem=send_sem.at[kind - 1, h, which],
            recv_sem=recv_sem.at[kind - 1, h, which],
            device_id={"blk": target},
            device_id_type=MESH,
        )

    def own_send(kind, h, which, target):
        return send(kind, h, which, (k_hbm, v_hbm)[which].at[:, cols(h)], kv_buf.at[kind, which, h], target)

    def pass_on(kind, held, h, which, target):
        return send(kind, h, which, kv_buf.at[held, which, h], kv_buf.at[kind, which, h], target)

    def far_send(h, which):
        return send(ALONG, h, which, fwd_buf.at[which, h], far_buf.at[1, which, h], along_to)

    def wait_for(kind, h, which):
        pass_on(kind, kind, h, which, sibling).wait_recv()

    width = w_hbm.shape[0]
    half = width // 2

    def w_place(r, col, core, part):
        index = 4 * r + 2 * col + core
        return pl.ds(pl.multiple_of(index * width + part * half, 32), half)

    def w_copy(source, place, sems, device):
        return pltpu.make_async_remote_copy(
            src_ref=source,
            dst_ref=w_buf.at[place],
            send_sem=sems[0],
            recv_sem=sems[1],
            device_id=device,
            device_id_type=MESH,
        )

    own_half = w_hbm.at[pl.ds(pl.multiple_of(g * half, 32), half)]

    def column(rel):
        return y if rel == 0 else 1 - y

    def w_z(rel, r, way, own=False):
        place = w_place(r, column(rel), c, g)
        return w_copy(
            own_half if own else w_buf.at[place], place,
            (wz_send.at[rel, r, way], wz_recv.at[rel, r]),
            {"blk": outer if way else inner},
        )

    def w_y(r, own=False):
        place = w_place(r, y, c, g)
        return w_copy(
            own_half if own else w_buf.at[place], place,
            (wy_send.at[r], wy_recv.at[r]), {"blk": across},
        )

    thin = half // SLICES

    def slice_rows(start, q):
        return pl.ds(pl.multiple_of(start + q * thin, 32), thin)

    def slice_place(r, col, part, q):
        return slice_rows((4 * r + 2 * col + 1) * width + part * half, q)

    def t_y(r, q, own=False):
        place = slice_place(r, y, g, q)
        return w_copy(
            w_hbm.at[slice_rows(g * half, q)] if own else w_buf.at[place], place,
            (ty_send.at[r, q], ty_recv.at[r, q]), {"blk": across},
        )

    def t_y_wait(r, q):
        place = slice_place(r, 1 - y, g, q)
        w_copy(w_buf.at[place], place, (ty_send.at[r, q], ty_recv.at[r, q]), {"blk": across}).wait_recv()

    def t_x(r, part, q):
        place = slice_place(r, 1 - y, part, q)
        return w_copy(w_buf.at[place], place, (tx_send.at[r, q], tx_recv.at[r, q]), {"groups": 1 - g})

    def t_s(r, part, q):
        place = slice_place(r, 1 - y, part, q)
        return w_copy(
            w_buf.at[place], place, (ts_send.at[part, r, q], ts_recv.at[part, r, q]), {"blk": sibling}
        )

    def w_x(rel, r, part):
        place = w_place(r, column(rel), c, part)
        return w_copy(
            w_buf.at[place], place, (wx_send.at[rel, r], wx_recv.at[rel, r]), {"groups": 1 - g}
        )

    def w_s(rel, r, part, own=False):
        place = w_place(r, column(rel), c, part)
        source = w_hbm.at[pl.ds(pl.multiple_of(part * half, 32), half)] if own else w_buf.at[place]
        return w_copy(
            source, place, (ws_send.at[part, rel, r], ws_recv.at[part, rel, r]), {"blk": sibling}
        )

    own_place = pl.ds(pl.multiple_of(s * width, 32), width)
    w_keep = pltpu.make_async_copy(w_hbm, w_buf.at[own_place], small_sem.at[1])
    mask_load = pltpu.make_async_copy(mask_hbm, mask_buf, small_sem.at[0])
    note = pltpu.make_async_remote_copy(
        src_ref=note_out,
        dst_ref=note_in,
        send_sem=note_sem.at[0],
        recv_sem=note_sem.at[1],
        device_id={"blk": along_from},
        device_id_type=MESH,
    )

    mask_load.start()
    barrier = pltpu.get_barrier_semaphore()
    peers = [{"blk": device} for device in (sibling, across, along_to, along_from)]
    peers.append({"groups": 1 - g})
    for device in peers:
        pl.semaphore_signal(barrier, inc=1, device_id=device, device_id_type=MESH)
    pl.semaphore_wait(barrier, len(peers))

    def begin_across(h, carry):
        for which in range(2):
            own_send(ACROSS, h, which, across).start()
        return carry

    def begin(h, carry):
        for which in range(2):
            own_send(SIBLING, h, which, sibling).start()
        for which in range(3):
            load(h, which).start()
        return carry

    begin_across(0, 0)
    w_z(0, z, 0, own=True).start()

    @pl.when(middle == 1)
    def _():
        w_z(0, z, 1, own=True).start()

    begin_across(1, 0)

    @pl.when(c == 0)
    def _():
        w_y(z, own=True).start()

    lax.fori_loop(2, LOOKAHEAD, begin_across, 0)
    lax.fori_loop(0, HEADS, begin, 0)
    w_keep.start()
    for part in range(2):
        w_s(0, z, part, own=True).start()

    mask_load.wait()
    base_across = jnp.where(y == 0, 4 * per_slab, 0)
    base_along = 4 * per_slab - base_across
    base_sibling = jnp.where(c == 0, 3 * per_slab, per_slab)
    base_relayed = 4 * per_slab - base_sibling

    def admitted(base):
        used = []
        for n in range(per_slab):
            value = mask_buf[0, base + n]
            for b in range(1, per_slab):
                value = jnp.maximum(value, mask_buf[b, base + n])
            used.append(value > 0)
        first = jnp.where(used[0], 0, jnp.where(used[1], 1, 2))
        second = jnp.where(used[3], 3, jnp.where(used[2], 2, 1))
        return first, second

    across_pick = admitted(base_across)
    along_pick = admitted(base_along)
    for n in range(2):
        level = jnp.full(note_out.shape[1:], along_pick[n].astype(jnp.float32), jnp.float32)
        note_out[n] = level.astype(jnp.bfloat16)
    note.start()

    def offset(value):
        return jnp.where(value > 0, 0.0, NEG).astype(jnp.float32)

    for b in range(per_slab):
        for n in range(per_slab):
            bias_buf[b, n] = offset(mask_buf[b, base_sibling + n])
            bias_buf[b, per_slab + n] = offset(mask_buf[b, base_relayed + n])
        for n in range(2):
            bias_buf[b, 2 * per_slab + n] = offset(mask_buf[b, base_across + across_pick[n]])
            bias_buf[b, 2 * per_slab + 2 + n] = offset(mask_buf[b, base_along + along_pick[n]])
    note.wait()

    def gather_far(kind, held, h, which, picks):
        piece = [kv_buf[held, which, h, n * BLOCK : (n + 1) * BLOCK, :] for n in range(per_slab)]
        first = lax.select(picks[0] == 0, piece[0], lax.select(picks[0] == 1, piece[1], piece[2]))
        second = lax.select(picks[1] == 3, piece[3], lax.select(picks[1] == 2, piece[2], piece[1]))
        far_buf[kind, which, h, :BLOCK, :] = first
        far_buf[kind, which, h, BLOCK:, :] = second

    def gather_forward(h, which):
        size = note_in.shape[1]
        first, second = note_in[0], note_in[1]
        for t in range(BLOCK // size):
            piece = [
                kv_buf[ACROSS, which, h, n * BLOCK + t * size : n * BLOCK + (t + 1) * size, :]
                for n in range(per_slab)
            ]
            fwd_buf[which, h, t * size : (t + 1) * size, :] = jnp.where(
                first == 0, piece[0], jnp.where(first == 1, piece[1], piece[2])
            )
            fwd_buf[which, h, BLOCK + t * size : BLOCK + (t + 1) * size, :] = jnp.where(
                second == 3, piece[3], jnp.where(second == 2, piece[2], piece[1])
            )

    def head_rows(h, part):
        first = pl.multiple_of(part * rows, rows)
        q = q_buf[h, pl.ds(first, rows), :]
        segments = [
            (kv_buf.at[OWN], tok, None),
            (kv_buf.at[SIBLING], tok, 0),
            (kv_buf.at[RELAYED], tok, per_slab),
            (far_buf.at[0], 2 * BLOCK, 2 * per_slab),
            (far_buf.at[1], 2 * BLOCK, 2 * per_slab + 2),
        ]
        peak = jnp.full((rows, BLOCK), NEG, jnp.float32)
        start = 0
        for ref, length, bias in segments:
            raw = nt_dot(q, ref[0, h]) * factor
            for n in range(length // BLOCK):
                col = start + n * BLOCK
                for b in range(blocks):
                    piece = raw[b * BLOCK : (b + 1) * BLOCK, n * BLOCK : (n + 1) * BLOCK]
                    if bias is not None:
                        piece = piece + bias_buf[part * blocks + b, bias + n]
                    score_buf[b * BLOCK : (b + 1) * BLOCK, col : col + BLOCK] = piece
                peak = jnp.maximum(peak, score_buf[:, col : col + BLOCK])
            start += length
        top = jnp.max(peak, axis=1, keepdims=True)
        mass = jnp.zeros((rows, BLOCK), jnp.float32)
        total = jnp.zeros((rows, head), jnp.float32)
        start = 0
        for ref, length, bias in segments:
            weights = jnp.exp2(score_buf[:, start : start + length] - top)
            for n in range(length // BLOCK):
                mass = mass + weights[:, n * BLOCK : (n + 1) * BLOCK]
            total = total + jnp.dot(
                weights.astype(jnp.bfloat16), ref[1, h], preferred_element_type=jnp.float32
            )
            start += length
        result = total / jnp.sum(mass, axis=1, keepdims=True)
        heads_ref[pl.ds(first, rows), cols(h)] = result.astype(jnp.bfloat16)

    def ready(h):
        for which in range(3):
            load(h, which).wait()
        for which in range(2):
            wait_for(SIBLING, h, which)

        @pl.when(late == 0)
        def _():
            for which in range(2):
                far_send(h, which).wait_recv()

        for which in range(2):
            wait_for(RELAYED, h, which)

    def relay(h, which):
        wait_for(ACROSS, h, which)

        @pl.when(late == 1)
        def _():
            pass_on(ALONG, ACROSS, h, which, along_to).start()

        @pl.when(late == 0)
        def _():
            gather_forward(h, which)
            far_send(h, which).start()
            pass_on(RELAYED, ACROSS, h, which, sibling).start()

        gather_far(0, ACROSS, h, which, across_pick)

    def relay_late(h, which):
        wait_for(ALONG, h, which)
        pass_on(RELAYED, ALONG, h, which, sibling).start()
        gather_far(1, ALONG, h, which, along_pick)

    def got(rel, r):
        w_x(rel, r, g).start()
        w_s(rel, r, g).start()

    def z_arrives(k, rel):
        r = row_of(k)
        w_z(rel, r, 0).wait_recv()

        @pl.when(middle == 1)
        def _():
            w_z(rel, r, 0 if k == 1 else 1).start()

        got(rel, r)

    def twin_arrives(k, rel):
        r = row_of(k)
        w_x(rel, r, 1 - g).wait_recv()
        w_s(rel, r, 1 - g).start()

    def at(i, end, mid, core):
        return pl.when((i == jnp.where(middle == 1, mid, end)) & (c == core))

    def weight_step(i):
        @at(i, 0, 0, 0)
        def _():
            w_y_wait_row(z)
            w_z(1, z, 0).start()

            @pl.when(middle == 1)
            def _():
                w_z(1, z, 1).start()

            got(1, z)

        for core, k, end, mid in ((0, 1, 0, 0), (0, 2, 1, 0), (0, 3, 3, 2), (1, 1, 1, 1), (1, 2, 2, 1), (1, 3, 6, 5)):

            @at(i, end, mid, core)
            def _():
                z_arrives(k, 0)

        for core, k, end, mid in ((0, 1, 2, 2), (0, 2, 3, 2), (0, 3, 5, 4), (1, 1, 3, 3), (1, 2, 4, 3), (1, 3, 8, 7)):

            @at(i, end, mid, core)
            def _():
                twin_arrives(k, 0)

        for k, end, mid in ((1, 1, 1), (2, 2, 1), (3, 4, 3)):

            @at(i, end, mid, 0)
            def _():
                z_arrives(k, 1)

        for k, end, mid in ((0, 2, 2), (1, 3, 3), (2, 4, 3), (3, 6, 5)):

            @at(i, end, mid, 0)
            def _():
                twin_arrives(k, 1)

        for k, when in ((0, 4), (1, 10), (2, 11), (3, 11)):

            @at(i, when, when, 1)
            def _():
                for q in range(SLICES):
                    t_y(row_of(k), q, own=k == 0).start()

        for k, when in ((0, 6), (1, 12), (2, 13)):

            @at(i, when, when, 1)
            def _():
                across_arrives(k)

    def w_y_wait_row(r):
        place = w_place(r, 1 - y, c, g)
        w_copy(
            w_buf.at[place], w_place(r, 1 - y, c, g), (wy_send.at[r], wy_recv.at[r]), {"blk": across}
        ).wait_recv()

    def across_arrives(k):
        r = row_of(k)
        for q in range(SLICES):
            t_y_wait(r, q)
            t_x(r, g, q).start()
            t_s(r, g, q).start()

    def step(i, carry):
        def part_step(part, carry):
            @pl.when(i < HEADS)
            def _():
                relay(i, part)

            @pl.when((i >= LAG - 1) & (i < HEADS + LAG - 1) & (late == 1))
            def _():
                relay_late(i - LAG + 1, part)

            @pl.when((i >= LAG) & (part == 0))
            def _():
                ready(i - LAG)

            @pl.when(i >= LAG)
            def _():
                head_rows(i - LAG, part)

            return carry

        lax.fori_loop(0, 2, part_step, 0)

        @pl.when(i + LOOKAHEAD < HEADS)
        def _():
            begin_across(i + LOOKAHEAD, 0)

        weight_step(i)
        return carry

    lax.fori_loop(0, HEADS + LAG, step, 0)

    w_keep.wait()
    chunk = 4 * width
    for k in range(4):
        r = row_of(k)

        @pl.when(c == 1)
        def _():
            if k + 1 == 3:
                across_arrives(3)
            for q in range(SLICES):
                t_x(r, 1 - g, q).wait_recv()
                t_s(r, 1 - g, q).start()

        for rel in range(2):
            for part in range(2):

                @pl.when((c == 1) | (rel == 0))
                def _():
                    place = w_place(r, column(rel), 1 - c, part)
                    w_copy(
                        w_buf.at[place], place,
                        (ws_send.at[part, rel, r], ws_recv.at[part, rel, r]), {"blk": sibling},
                    ).wait_recv()

        @pl.when(c == 0)
        def _():
            for part in range(2):
                for q in range(SLICES):
                    t_s(r, part, q).wait_recv()

        def tile(t, carry):
            place = pl.ds(pl.multiple_of(r * 4 * width + t * chunk, 128), chunk)
            out_ref[:, place] = nt_dot(heads_ref[...], w_buf[place, :]).astype(out_ref.dtype)
            return carry

        lax.fori_loop(0, 4 * width // chunk, tile, 0)

    def finish(h, carry):
        for kind in (ACROSS, SIBLING, RELAYED):
            for which in range(2):
                own_send(kind, h, which, sibling).wait_send()

        @pl.when(late == 1)
        def _():
            for which in range(2):
                own_send(ALONG, h, which, sibling).wait_send()

        @pl.when(late == 0)
        def _():
            for which in range(2):
                far_send(h, which).wait_send()

        return carry

    lax.fori_loop(0, HEADS, finish, 0)

    def z_sent(rel):
        w_z(rel, z, 0).wait_send()

        @pl.when(middle == 1)
        def _():
            w_z(rel, z, 1).wait_send()
            w_z(rel, row_of(1), 0).wait_send()
            w_z(rel, row_of(2), 1).wait_send()
            w_z(rel, row_of(3), 1).wait_send()

    z_sent(0)

    @pl.when(c == 0)
    def _():
        z_sent(1)
        w_y(z).wait_send()

    for k in range(4):
        r = row_of(k)
        for rel in range(2):

            @pl.when((c == 0) | (rel == 0))
            def _():
                if k or rel:
                    w_x(rel, r, g).wait_send()
                for part in range(2):
                    w_s(rel, r, part).wait_send()

        @pl.when(c == 1)
        def _():
            for q in range(SLICES):
                t_y(r, q).wait_send()
                t_x(r, g, q).wait_send()
                for part in range(2):
                    t_s(r, part, q).wait_send()


def fused(queries, key_rows, value_rows, block_mask, weight):
    tok, feat = queries.shape
    head = feat // HEADS
    width = 16 * weight.shape[0]
    per_slab = tok // BLOCK
    columns = 3 * tok + 4 * BLOCK
    dma = pltpu.SemaphoreType.DMA
    bf16, f32 = jnp.bfloat16, jnp.float32
    scratch = [
        pltpu.VMEM((HEADS, tok, head), bf16),
        pltpu.VMEM((5, 2, HEADS, tok, head), bf16),
        pltpu.VMEM((2, 2, HEADS, 2 * BLOCK, head), bf16),
        pltpu.VMEM((2, HEADS, 2 * BLOCK, head), bf16),
        pltpu.VMEM((min(256, tok), columns), f32),
        pltpu.VMEM((tok, feat), bf16),
        pltpu.VMEM((width, feat), bf16),
        pltpu.SMEM(block_mask.shape, jnp.int32),
        pltpu.SMEM((per_slab, 2 * per_slab + 4), f32),
        pltpu.VMEM((2, 16, head), bf16),
        pltpu.VMEM((2, 16, head), bf16),
        dma((4, HEADS, 2)),
        dma((4, HEADS, 2)),
        dma((HEADS, 3)),
        dma((2,)),
        dma((2,)),
        dma((2, 4, 2)),
        dma((2, 4)),
        dma((4,)),
        dma((4,)),
        dma((2, 4)),
        dma((2, 4)),
        dma((2, 2, 4)),
        dma((2, 2, 4)),
        dma((4, SLICES)),
        dma((4, SLICES)),
        dma((4, SLICES)),
        dma((4, SLICES)),
        dma((2, 4, SLICES)),
        dma((2, 4, SLICES)),
    ]
    return pl.pallas_call(
        fused_kernel,
        out_shape=jax.ShapeDtypeStruct((tok, width), bf16),
        in_specs=[pl.BlockSpec(memory_space=pl.ANY)] * 5,
        out_specs=pl.BlockSpec(memory_space=pltpu.VMEM),
        scratch_shapes=scratch,
        compiler_params=pltpu.CompilerParams(
            collective_id=0, has_side_effects=True, vmem_limit_bytes=60 * 2**20
        ),
    )(queries, key_rows, value_rows, block_mask, weight)


def attend_kernel(slabs, q_hbm, k_hbm, v_hbm, bias_ref, heads_ref, q_buf, kv_buf, score_buf, send_sem, recv_sem, load_sem):
    tok, feat = q_hbm.shape
    head = feat // HEADS
    rows = min(256, tok)
    blocks = rows // BLOCK
    factor = math.log2(math.e) / math.sqrt(head)
    s = lax.axis_index("blk")
    c = lax.rem(s, 2)
    y = lax.rem(s // 2, 2)
    sibling = s + 1 - 2 * c
    across = s + 2 - 4 * y
    along_to = lax.rem(s + 4 - 8 * y + slabs, slabs)
    along_from = lax.rem(s - 4 + 8 * y + slabs, slabs)
    late = lax.rem(y + c, 2)

    def cols(h):
        return pl.ds(pl.multiple_of(h * head, head), head)

    def load(h, which):
        src = (k_hbm, v_hbm, q_hbm)[which]
        dst = q_buf.at[h] if which == 2 else kv_buf.at[OWN, which, h]
        return pltpu.make_async_copy(src.at[:, cols(h)], dst, load_sem.at[h, which])

    def send(kind, h, which, source, target):
        return pltpu.make_async_remote_copy(
            src_ref=source,
            dst_ref=kv_buf.at[kind, which, h],
            send_sem=send_sem.at[kind - 1, h, which],
            recv_sem=recv_sem.at[kind - 1, h, which],
            device_id={"blk": target},
            device_id_type=MESH,
        )

    def own_send(kind, h, which, target):
        return send(kind, h, which, (k_hbm, v_hbm)[which].at[:, cols(h)], target)

    def pass_on(kind, held, h, which, target):
        return send(kind, h, which, kv_buf.at[held, which, h], target)

    def wait_for(kind, h, which):
        own_send(kind, h, which, sibling).wait_recv()

    def arrived(kind, h):
        for which in range(2):
            wait_for(kind, h, which)

    barrier = pltpu.get_barrier_semaphore()
    peers = (sibling, across, along_to, along_from)
    for device in peers:
        pl.semaphore_signal(barrier, inc=1, device_id={"blk": device}, device_id_type=MESH)
    pl.semaphore_wait(barrier, len(peers))

    def begin_across(h, carry):
        for which in range(2):
            own_send(ACROSS, h, which, across).start()
        return carry

    def begin(h, carry):
        for which in range(2):
            own_send(SIBLING, h, which, sibling).start()
        for which in range(3):
            load(h, which).start()
        return carry

    lax.fori_loop(0, LOOKAHEAD, begin_across, 0)
    lax.fori_loop(0, HEADS, begin, 0)

    def head_rows(h, part):
        first = pl.multiple_of(part * rows, rows)
        q = q_buf[h, pl.ds(first, rows), :]
        peak = jnp.full((rows, 128), NEG, jnp.float32)
        for j in range(5):
            raw = nt_dot(q, kv_buf[j, 0, h]) * factor
            for b in range(blocks):
                for n in range(tok // BLOCK):
                    col = j * tok + n * BLOCK
                    piece = raw[b * BLOCK : (b + 1) * BLOCK, n * BLOCK : (n + 1) * BLOCK]
                    piece = piece + bias_ref[part * blocks + b, :, col : col + BLOCK]
                    score_buf[b * BLOCK : (b + 1) * BLOCK, col : col + BLOCK] = piece
            for n in range(tok // BLOCK):
                col = j * tok + n * BLOCK
                peak = jnp.maximum(peak, score_buf[:, col : col + BLOCK])
        top = jnp.max(peak, axis=1, keepdims=True)
        mass = jnp.zeros((rows, 128), jnp.float32)
        total = jnp.zeros((rows, head), jnp.float32)
        for j in range(5):
            weights = jnp.exp2(score_buf[:, j * tok : (j + 1) * tok] - top)
            for n in range(tok // BLOCK):
                mass = mass + weights[:, n * BLOCK : (n + 1) * BLOCK]
            total = total + jnp.dot(
                weights.astype(jnp.bfloat16), kv_buf[j, 1, h], preferred_element_type=jnp.float32
            )
        result = total / jnp.sum(mass, axis=1, keepdims=True)
        heads_ref[pl.ds(first, rows), cols(h)] = result.astype(jnp.bfloat16)

    def compute(h):
        for which in range(3):
            load(h, which).wait()
        arrived(SIBLING, h)

        @pl.when(late == 0)
        def _():
            arrived(ALONG, h)

        arrived(RELAYED, h)

        def part_step(part, carry):
            head_rows(h, part)
            return carry

        lax.fori_loop(0, tok // rows, part_step, 0)

    def relay_late(h):
        for which in range(2):
            wait_for(ALONG, h, which)
            pass_on(RELAYED, ALONG, h, which, sibling).start()

    def step(i, carry):
        @pl.when((i >= 2) & (i < HEADS))
        def _():
            compute(i - 2)

        @pl.when(i < HEADS)
        def _():
            for which in range(2):
                wait_for(ACROSS, i, which)
                pass_on(ALONG, ACROSS, i, which, along_to).start()

                @pl.when(late == 0)
                def _():
                    pass_on(RELAYED, ACROSS, i, which, sibling).start()

        @pl.when(i + LOOKAHEAD < HEADS)
        def _():
            begin_across(i + LOOKAHEAD, 0)

        @pl.when((i >= 1) & (i < HEADS + 1) & (late == 1))
        def _():
            relay_late(i - 1)

        @pl.when(i >= HEADS)
        def _():
            compute(i - 2)

        return carry

    lax.fori_loop(0, HEADS + 2, step, 0)

    def finish(h, carry):
        for kind in (ACROSS, ALONG, SIBLING, RELAYED):
            for which in range(2):
                own_send(kind, h, which, sibling).wait_send()
        return carry

    lax.fori_loop(0, HEADS, finish, 0)


def attend(slabs, queries, key_rows, value_rows, bias):
    tok, feat = queries.shape
    head = feat // HEADS
    return pl.pallas_call(
        functools.partial(attend_kernel, slabs),
        out_shape=jax.ShapeDtypeStruct((tok, feat), jnp.bfloat16),
        in_specs=[pl.BlockSpec(memory_space=pl.ANY)] * 3 + [pl.BlockSpec(memory_space=pltpu.VMEM)],
        out_specs=pl.BlockSpec(memory_space=pltpu.VMEM),
        scratch_shapes=[
            pltpu.VMEM((HEADS, tok, head), jnp.bfloat16),
            pltpu.VMEM((5, 2, HEADS, tok, head), jnp.bfloat16),
            pltpu.VMEM((min(256, tok), 5 * tok), jnp.float32),
            pltpu.SemaphoreType.DMA((4, HEADS, 2)),
            pltpu.SemaphoreType.DMA((4, HEADS, 2)),
            pltpu.SemaphoreType.DMA((HEADS, 3)),
        ],
        compiler_params=pltpu.CompilerParams(
            collective_id=0, has_side_effects=True, vmem_limit_bytes=60 * 2**20
        ),
    )(queries, key_rows, value_rows, bias)


def local(slabs, groups, queries, key_rows, value_rows, block_mask, out_weight):
    per_slab = queries.shape[0] // BLOCK
    if groups == 2 and slabs == 16 and per_slab == 4 and out_weight.shape[1] % 64 == 0:
        return fused(queries, key_rows, value_rows, block_mask, out_weight.T)
    s = lax.axis_index("blk")
    c = s % 2
    y = (s // 2) % 2
    table = jnp.where(block_mask > 0, 0.0, NEG).astype(jnp.float32)
    table = table.reshape(block_mask.shape[0], 2 * RADIUS + 1, per_slab)
    back2, back1, own, next1, next2 = (table[:, d] for d in range(5))
    ordered = jnp.concatenate(
        (
            own,
            jnp.where(y == 0, next2, back2),
            jnp.where(y == 0, back2, next2),
            jnp.where(c == 0, next1, back1),
            jnp.where(c == 0, back1, next1),
        ),
        axis=1,
    )
    bias = jnp.repeat(ordered, BLOCK, axis=1)[:, None, :]
    attention = attend(slabs, queries, key_rows, value_rows, bias)
    weight = lax.all_gather(out_weight, "blk", axis=1, tiled=True)
    return jnp.dot(attention, weight, preferred_element_type=jnp.float32).astype(jnp.bfloat16)


def solution(mesh):
    in_specs = (
        P(("groups", "blk"), None),
        P(("groups", "blk"), None),
        P(("groups", "blk"), None),
        P("blk", None),
        P(None, "blk"),
    )
    out_specs = P(("groups", "blk"), None)
    body = functools.partial(local, mesh.shape["blk"], mesh.shape["groups"])
    return jax.shard_map(body, mesh=mesh, in_specs=in_specs, out_specs=out_specs, check_vma=False)
```

```python
import functools
import math

import jax
import jax.numpy as jnp
from jax import lax
from jax.experimental import pallas as pl
from jax.experimental.pallas import tpu as pltpu
from jax.sharding import PartitionSpec as P

HEADS = 12
BLOCK = 128
RADIUS = 2
NEG = -1e30
OWN, ACROSS, ALONG, SIBLING, RELAYED = range(5)
MESH = pl.DeviceIdType.MESH


def nt_dot(a, b):
    return lax.dot_general(a, b, (((1,), (1,)), ((), ())), preferred_element_type=jnp.float32)


LOOKAHEAD = 4
LAG = 3
SLICES = 1

def fused_kernel(
    q_hbm, k_hbm, v_hbm, mask_hbm, w_hbm, out_ref,
    q_buf, kv_buf, far_buf, fwd_buf, score_buf, heads_ref, w_buf, mask_buf, bias_buf, note_out, note_in,
    send_sem, recv_sem, load_sem, small_sem, note_sem,
    wz_send, wz_recv, wy_send, wy_recv, wx_send, wx_recv, ws_send, ws_recv,
    ty_send, ty_recv, tx_send, tx_recv, ts_send, ts_recv,
):
    tok, feat = q_hbm.shape
    head = feat // HEADS
    rows = min(256, tok)
    blocks = rows // BLOCK
    per_slab = tok // BLOCK
    factor = math.log2(math.e) / math.sqrt(head)
    slabs = 16
    s = lax.axis_index("blk")
    g = lax.axis_index("groups")
    c = lax.rem(s, 2)
    y = lax.rem(s // 2, 2)
    z = s // 4
    sibling = s + 1 - 2 * c
    across = s + 2 - 4 * y
    along_to = lax.rem(s + 4 - 8 * y + slabs, slabs)
    along_from = lax.rem(s - 4 + 8 * y + slabs, slabs)
    late = lax.rem(y + c, 2)
    inward = jnp.where(z < 2, 1, -1)
    middle = jnp.where((z == 1) | (z == 2), 1, 0)
    inner = s + 4 * inward
    outer = s - 4 * inward

    def row_of(k):
        back = 0 if k == 0 else 2 if k == 1 else 1
        return z + inward * (k - middle * back)

    def cols(h):
        return pl.ds(pl.multiple_of(h * head, head), head)

    def load(h, which):
        src = (k_hbm, v_hbm, q_hbm)[which]
        dst = q_buf.at[h] if which == 2 else kv_buf.at[OWN, which, h]
        return pltpu.make_async_copy(src.at[:, cols(h)], dst, load_sem.at[h, which])

    def send(kind, h, which, source, place, target):
        return pltpu.make_async_remote_copy(
            src_ref=source,
            dst_ref=place,
            send_sem=send_sem.at[kind - 1, h, which],
            recv_sem=recv_sem.at[kind - 1, h, which],
            device_id={"blk": target},
            device_id_type=MESH,
        )

    def own_send(kind, h, which, target):
        return send(kind, h, which, (k_hbm, v_hbm)[which].at[:, cols(h)], kv_buf.at[kind, which, h], target)

    def pass_on(kind, held, h, which, target):
        return send(kind, h, which, kv_buf.at[held, which, h], kv_buf.at[kind, which, h], target)

    def far_send(h, which):
        return send(ALONG, h, which, fwd_buf.at[which, h], far_buf.at[1, which, h], along_to)

    def wait_for(kind, h, which):
        pass_on(kind, kind, h, which, sibling).wait_recv()

    width = w_hbm.shape[0]
    half = width // 2

    def w_place(r, col, core, part):
        index = 4 * r + 2 * col + core
        return pl.ds(pl.multiple_of(index * width + part * half, 32), half)

    def w_copy(source, place, sems, device):
        return pltpu.make_async_remote_copy(
            src_ref=source,
            dst_ref=w_buf.at[place],
            send_sem=sems[0],
            recv_sem=sems[1],
            device_id=device,
            device_id_type=MESH,
        )

    own_half = w_hbm.at[pl.ds(pl.multiple_of(g * half, 32), half)]

    def column(rel):
        return y if rel == 0 else 1 - y

    def w_z(rel, r, way, own=False):
        place = w_place(r, column(rel), c, g)
        return w_copy(
            own_half if own else w_buf.at[place], place,
            (wz_send.at[rel, r, way], wz_recv.at[rel, r]),
            {"blk": outer if way else inner},
        )

    def w_y(r, own=False):
        place = w_place(r, y, c, g)
        return w_copy(
            own_half if own else w_buf.at[place], place,
            (wy_send.at[r], wy_recv.at[r]), {"blk": across},
        )

    thin = half // SLICES

    def slice_rows(start, q):
        return pl.ds(pl.multiple_of(start + q * thin, 32), thin)

    def slice_place(r, col, part, q):
        return slice_rows((4 * r + 2 * col + 1) * width + part * half, q)

    def t_y(r, q, own=False):
        place = slice_place(r, y, g, q)
        return w_copy(
            w_hbm.at[slice_rows(g * half, q)] if own else w_buf.at[place], place,
            (ty_send.at[r, q], ty_recv.at[r, q]), {"blk": across},
        )

    def t_y_wait(r, q):
        place = slice_place(r, 1 - y, g, q)
        w_copy(w_buf.at[place], place, (ty_send.at[r, q], ty_recv.at[r, q]), {"blk": across}).wait_recv()

    def t_x(r, part, q):
        place = slice_place(r, 1 - y, part, q)
        return w_copy(w_buf.at[place], place, (tx_send.at[r, q], tx_recv.at[r, q]), {"groups": 1 - g})

    def t_s(r, part, q):
        place = slice_place(r, 1 - y, part, q)
        return w_copy(
            w_buf.at[place], place, (ts_send.at[part, r, q], ts_recv.at[part, r, q]), {"blk": sibling}
        )

    def w_x(rel, r, part):
        place = w_place(r, column(rel), c, part)
        return w_copy(
            w_buf.at[place], place, (wx_send.at[rel, r], wx_recv.at[rel, r]), {"groups": 1 - g}
        )

    def w_s(rel, r, part, own=False):
        place = w_place(r, column(rel), c, part)
        source = w_hbm.at[pl.ds(pl.multiple_of(part * half, 32), half)] if own else w_buf.at[place]
        return w_copy(
            source, place, (ws_send.at[part, rel, r], ws_recv.at[part, rel, r]), {"blk": sibling}
        )

    own_place = pl.ds(pl.multiple_of(s * width, 32), width)
    w_keep = pltpu.make_async_copy(w_hbm, w_buf.at[own_place], small_sem.at[1])
    mask_load = pltpu.make_async_copy(mask_hbm, mask_buf, small_sem.at[0])
    note = pltpu.make_async_remote_copy(
        src_ref=note_out,
        dst_ref=note_in,
        send_sem=note_sem.at[0],
        recv_sem=note_sem.at[1],
        device_id={"blk": along_from},
        device_id_type=MESH,
    )

    mask_load.start()
    barrier = pltpu.get_barrier_semaphore()
    peers = [{"blk": device} for device in (sibling, across, along_to, along_from)]
    peers.append({"groups": 1 - g})
    for device in peers:
        pl.semaphore_signal(barrier, inc=1, device_id=device, device_id_type=MESH)
    pl.semaphore_wait(barrier, len(peers))

    def begin_across(h, carry):
        for which in range(2):
            own_send(ACROSS, h, which, across).start()
        return carry

    def begin(h, carry):
        for which in range(2):
            own_send(SIBLING, h, which, sibling).start()
        for which in range(3):
            load(h, which).start()
        return carry

    begin_across(0, 0)
    w_z(0, z, 0, own=True).start()

    @pl.when(middle == 1)
    def _():
        w_z(0, z, 1, own=True).start()

    begin_across(1, 0)

    @pl.when(c == 0)
    def _():
        w_y(z, own=True).start()

    lax.fori_loop(2, LOOKAHEAD, begin_across, 0)
    lax.fori_loop(0, HEADS, begin, 0)
    w_keep.start()
    for part in range(2):
        w_s(0, z, part, own=True).start()

    mask_load.wait()
    base_across = jnp.where(y == 0, 4 * per_slab, 0)
    base_along = 4 * per_slab - base_across
    base_sibling = jnp.where(c == 0, 3 * per_slab, per_slab)
    base_relayed = 4 * per_slab - base_sibling

    def admitted(base):
        used = []
        for n in range(per_slab):
            value = mask_buf[0, base + n]
            for b in range(1, per_slab):
                value = jnp.maximum(value, mask_buf[b, base + n])
            used.append(value > 0)
        first = jnp.where(used[0], 0, jnp.where(used[1], 1, 2))
        second = jnp.where(used[3], 3, jnp.where(used[2], 2, 1))
        return first, second

    across_pick = admitted(base_across)
    along_pick = admitted(base_along)
    for n in range(2):
        level = jnp.full(note_out.shape[1:], along_pick[n].astype(jnp.float32), jnp.float32)
        note_out[n] = level.astype(jnp.bfloat16)
    note.start()

    def offset(value):
        return jnp.where(value > 0, 0.0, NEG).astype(jnp.float32)

    for b in range(per_slab):
        for n in range(per_slab):
            bias_buf[b, n] = offset(mask_buf[b, base_sibling + n])
            bias_buf[b, per_slab + n] = offset(mask_buf[b, base_relayed + n])
        for n in range(2):
            bias_buf[b, 2 * per_slab + n] = offset(mask_buf[b, base_across + across_pick[n]])
            bias_buf[b, 2 * per_slab + 2 + n] = offset(mask_buf[b, base_along + along_pick[n]])
    note.wait()

    def gather_far(kind, held, h, which, picks):
        piece = [kv_buf[held, which, h, n * BLOCK : (n + 1) * BLOCK, :] for n in range(per_slab)]
        first = lax.select(picks[0] == 0, piece[0], lax.select(picks[0] == 1, piece[1], piece[2]))
        second = lax.select(picks[1] == 3, piece[3], lax.select(picks[1] == 2, piece[2], piece[1]))
        far_buf[kind, which, h, :BLOCK, :] = first
        far_buf[kind, which, h, BLOCK:, :] = second

    def gather_forward(h, which):
        size = note_in.shape[1]
        first, second = note_in[0], note_in[1]
        for t in range(BLOCK // size):
            piece = [
                kv_buf[ACROSS, which, h, n * BLOCK + t * size : n * BLOCK + (t + 1) * size, :]
                for n in range(per_slab)
            ]
            fwd_buf[which, h, t * size : (t + 1) * size, :] = jnp.where(
                first == 0, piece[0], jnp.where(first == 1, piece[1], piece[2])
            )
            fwd_buf[which, h, BLOCK + t * size : BLOCK + (t + 1) * size, :] = jnp.where(
                second == 3, piece[3], jnp.where(second == 2, piece[2], piece[1])
            )

    def head_rows(h, part):
        first = pl.multiple_of(part * rows, rows)
        q = q_buf[h, pl.ds(first, rows), :]
        segments = [
            (kv_buf.at[OWN], tok, None),
            (kv_buf.at[SIBLING], tok, 0),
            (kv_buf.at[RELAYED], tok, per_slab),
            (far_buf.at[0], 2 * BLOCK, 2 * per_slab),
            (far_buf.at[1], 2 * BLOCK, 2 * per_slab + 2),
        ]
        peak = jnp.full((rows, BLOCK), NEG, jnp.float32)
        start = 0
        for ref, length, bias in segments:
            raw = nt_dot(q, ref[0, h]) * factor
            for n in range(length // BLOCK):
                col = start + n * BLOCK
                for b in range(blocks):
                    piece = raw[b * BLOCK : (b + 1) * BLOCK, n * BLOCK : (n + 1) * BLOCK]
                    if bias is not None:
                        piece = piece + bias_buf[part * blocks + b, bias + n]
                    score_buf[b * BLOCK : (b + 1) * BLOCK, col : col + BLOCK] = piece
                peak = jnp.maximum(peak, score_buf[:, col : col + BLOCK])
            start += length
        top = jnp.max(peak, axis=1, keepdims=True)
        mass = jnp.zeros((rows, BLOCK), jnp.float32)
        total = jnp.zeros((rows, head), jnp.float32)
        start = 0
        for ref, length, bias in segments:
            weights = jnp.exp2(score_buf[:, start : start + length] - top)
            for n in range(length // BLOCK):
                mass = mass + weights[:, n * BLOCK : (n + 1) * BLOCK]
            total = total + jnp.dot(
                weights.astype(jnp.bfloat16), ref[1, h], preferred_element_type=jnp.float32
            )
            start += length
        result = total / jnp.sum(mass, axis=1, keepdims=True)
        heads_ref[pl.ds(first, rows), cols(h)] = result.astype(jnp.bfloat16)

    def ready(h):
        for which in range(3):
            load(h, which).wait()
        for which in range(2):
            wait_for(SIBLING, h, which)

        @pl.when(late == 0)
        def _():
            for which in range(2):
                far_send(h, which).wait_recv()

        for which in range(2):
            wait_for(RELAYED, h, which)

    def relay(h, which):
        wait_for(ACROSS, h, which)

        @pl.when(late == 1)
        def _():
            pass_on(ALONG, ACROSS, h, which, along_to).start()

        @pl.when(late == 0)
        def _():
            gather_forward(h, which)
            far_send(h, which).start()
            pass_on(RELAYED, ACROSS, h, which, sibling).start()

        gather_far(0, ACROSS, h, which, across_pick)

    def relay_late(h, which):
        wait_for(ALONG, h, which)
        pass_on(RELAYED, ALONG, h, which, sibling).start()
        gather_far(1, ALONG, h, which, along_pick)

    def got(rel, r):
        w_x(rel, r, g).start()
        w_s(rel, r, g).start()

    def z_arrives(k, rel):
        r = row_of(k)
        w_z(rel, r, 0).wait_recv()

        @pl.when(middle == 1)
        def _():
            w_z(rel, r, 0 if k == 1 else 1).start()

        got(rel, r)

    def twin_arrives(k, rel):
        r = row_of(k)
        w_x(rel, r, 1 - g).wait_recv()
        w_s(rel, r, 1 - g).start()

    def at(i, end, mid, core):
        return pl.when((i == jnp.where(middle == 1, mid, end)) & (c == core))

    def weight_step(i):
        @at(i, 0, 0, 0)
        def _():
            w_y_wait_row(z)
            w_z(1, z, 0).start()

            @pl.when(middle == 1)
            def _():
                w_z(1, z, 1).start()

            got(1, z)

        for core, k, end, mid in ((0, 1, 0, 0), (0, 2, 1, 0), (0, 3, 3, 2), (1, 1, 1, 1), (1, 2, 2, 1), (1, 3, 6, 5)):

            @at(i, end, mid, core)
            def _():
                z_arrives(k, 0)

        for core, k, end, mid in ((0, 1, 2, 2), (0, 2, 3, 2), (0, 3, 5, 4), (1, 1, 3, 3), (1, 2, 4, 3), (1, 3, 8, 7)):

            @at(i, end, mid, core)
            def _():
                twin_arrives(k, 0)

        for k, end, mid in ((1, 1, 1), (2, 2, 1), (3, 4, 3)):

            @at(i, end, mid, 0)
            def _():
                z_arrives(k, 1)

        for k, end, mid in ((0, 2, 2), (1, 3, 3), (2, 4, 3), (3, 6, 5)):

            @at(i, end, mid, 0)
            def _():
                twin_arrives(k, 1)

        for k, when in ((0, 4), (1, 10), (2, 11), (3, 11)):

            @at(i, when, when, 1)
            def _():
                for q in range(SLICES):
                    t_y(row_of(k), q, own=k == 0).start()

        for k, when in ((0, 6), (1, 12), (2, 13)):

            @at(i, when, when, 1)
            def _():
                across_arrives(k)

    def w_y_wait_row(r):
        place = w_place(r, 1 - y, c, g)
        w_copy(
            w_buf.at[place], w_place(r, 1 - y, c, g), (wy_send.at[r], wy_recv.at[r]), {"blk": across}
        ).wait_recv()

    def across_arrives(k):
        r = row_of(k)
        for q in range(SLICES):
            t_y_wait(r, q)
            t_x(r, g, q).start()
            t_s(r, g, q).start()

    def step(i, carry):
        def part_step(part, carry):
            @pl.when(i < HEADS)
            def _():
                relay(i, part)

            @pl.when((i >= LAG - 1) & (i < HEADS + LAG - 1) & (late == 1))
            def _():
                relay_late(i - LAG + 1, part)

            @pl.when((i >= LAG) & (part == 0))
            def _():
                ready(i - LAG)

            @pl.when(i >= LAG)
            def _():
                head_rows(i - LAG, part)

            return carry

        lax.fori_loop(0, 2, part_step, 0)

        @pl.when(i + LOOKAHEAD < HEADS)
        def _():
            begin_across(i + LOOKAHEAD, 0)

        weight_step(i)
        return carry

    lax.fori_loop(0, HEADS + LAG, step, 0)

    w_keep.wait()
    chunk = 4 * width
    for k in range(4):
        r = row_of(k)

        @pl.when(c == 1)
        def _():
            if k == 1:
                across_arrives(3)
            for q in range(SLICES):
                t_x(r, 1 - g, q).wait_recv()
                t_s(r, 1 - g, q).start()

        for rel in range(2):
            for part in range(2):

                @pl.when((c == 1) | (rel == 0))
                def _():
                    place = w_place(r, column(rel), 1 - c, part)
                    w_copy(
                        w_buf.at[place], place,
                        (ws_send.at[part, rel, r], ws_recv.at[part, rel, r]), {"blk": sibling},
                    ).wait_recv()

        @pl.when(c == 0)
        def _():
            for part in range(2):
                for q in range(SLICES):
                    t_s(r, part, q).wait_recv()

        def tile(t, carry):
            place = pl.ds(pl.multiple_of(r * 4 * width + t * chunk, 128), chunk)
            out_ref[:, place] = nt_dot(heads_ref[...], w_buf[place, :]).astype(out_ref.dtype)
            return carry

        lax.fori_loop(0, 4 * width // chunk, tile, 0)

    def finish(h, carry):
        for kind in (ACROSS, SIBLING, RELAYED):
            for which in range(2):
                own_send(kind, h, which, sibling).wait_send()

        @pl.when(late == 1)
        def _():
            for which in range(2):
                own_send(ALONG, h, which, sibling).wait_send()

        @pl.when(late == 0)
        def _():
            for which in range(2):
                far_send(h, which).wait_send()

        return carry

    lax.fori_loop(0, HEADS, finish, 0)

    def z_sent(rel):
        w_z(rel, z, 0).wait_send()

        @pl.when(middle == 1)
        def _():
            w_z(rel, z, 1).wait_send()
            w_z(rel, row_of(1), 0).wait_send()
            w_z(rel, row_of(2), 1).wait_send()
            w_z(rel, row_of(3), 1).wait_send()

    z_sent(0)

    @pl.when(c == 0)
    def _():
        z_sent(1)
        w_y(z).wait_send()

    for k in range(4):
        r = row_of(k)
        for rel in range(2):

            @pl.when((c == 0) | (rel == 0))
            def _():
                if k or rel:
                    w_x(rel, r, g).wait_send()
                for part in range(2):
                    w_s(rel, r, part).wait_send()

        @pl.when(c == 1)
        def _():
            for q in range(SLICES):
                t_y(r, q).wait_send()
                t_x(r, g, q).wait_send()
                for part in range(2):
                    t_s(r, part, q).wait_send()


def fused(queries, key_rows, value_rows, block_mask, weight):
    tok, feat = queries.shape
    head = feat // HEADS
    width = 16 * weight.shape[0]
    per_slab = tok // BLOCK
    columns = 3 * tok + 4 * BLOCK
    dma = pltpu.SemaphoreType.DMA
    bf16, f32 = jnp.bfloat16, jnp.float32
    scratch = [
        pltpu.VMEM((HEADS, tok, head), bf16),
        pltpu.VMEM((5, 2, HEADS, tok, head), bf16),
        pltpu.VMEM((2, 2, HEADS, 2 * BLOCK, head), bf16),
        pltpu.VMEM((2, HEADS, 2 * BLOCK, head), bf16),
        pltpu.VMEM((min(256, tok), columns), f32),
        pltpu.VMEM((tok, feat), bf16),
        pltpu.VMEM((width, feat), bf16),
        pltpu.SMEM(block_mask.shape, jnp.int32),
        pltpu.SMEM((per_slab, 2 * per_slab + 4), f32),
        pltpu.VMEM((2, 16, head), bf16),
        pltpu.VMEM((2, 16, head), bf16),
        dma((4, HEADS, 2)),
        dma((4, HEADS, 2)),
        dma((HEADS, 3)),
        dma((2,)),
        dma((2,)),
        dma((2, 4, 2)),
        dma((2, 4)),
        dma((4,)),
        dma((4,)),
        dma((2, 4)),
        dma((2, 4)),
        dma((2, 2, 4)),
        dma((2, 2, 4)),
        dma((4, SLICES)),
        dma((4, SLICES)),
        dma((4, SLICES)),
        dma((4, SLICES)),
        dma((2, 4, SLICES)),
        dma((2, 4, SLICES)),
    ]
    return pl.pallas_call(
        fused_kernel,
        out_shape=jax.ShapeDtypeStruct((tok, width), bf16),
        in_specs=[pl.BlockSpec(memory_space=pl.ANY)] * 5,
        out_specs=pl.BlockSpec(memory_space=pltpu.VMEM),
        scratch_shapes=scratch,
        compiler_params=pltpu.CompilerParams(
            collective_id=0, has_side_effects=True, vmem_limit_bytes=60 * 2**20
        ),
    )(queries, key_rows, value_rows, block_mask, weight)


def attend_kernel(slabs, q_hbm, k_hbm, v_hbm, bias_ref, heads_ref, q_buf, kv_buf, score_buf, send_sem, recv_sem, load_sem):
    tok, feat = q_hbm.shape
    head = feat // HEADS
    rows = min(256, tok)
    blocks = rows // BLOCK
    factor = math.log2(math.e) / math.sqrt(head)
    s = lax.axis_index("blk")
    c = lax.rem(s, 2)
    y = lax.rem(s // 2, 2)
    sibling = s + 1 - 2 * c
    across = s + 2 - 4 * y
    along_to = lax.rem(s + 4 - 8 * y + slabs, slabs)
    along_from = lax.rem(s - 4 + 8 * y + slabs, slabs)
    late = lax.rem(y + c, 2)

    def cols(h):
        return pl.ds(pl.multiple_of(h * head, head), head)

    def load(h, which):
        src = (k_hbm, v_hbm, q_hbm)[which]
        dst = q_buf.at[h] if which == 2 else kv_buf.at[OWN, which, h]
        return pltpu.make_async_copy(src.at[:, cols(h)], dst, load_sem.at[h, which])

    def send(kind, h, which, source, target):
        return pltpu.make_async_remote_copy(
            src_ref=source,
            dst_ref=kv_buf.at[kind, which, h],
            send_sem=send_sem.at[kind - 1, h, which],
            recv_sem=recv_sem.at[kind - 1, h, which],
            device_id={"blk": target},
            device_id_type=MESH,
        )

    def own_send(kind, h, which, target):
        return send(kind, h, which, (k_hbm, v_hbm)[which].at[:, cols(h)], target)

    def pass_on(kind, held, h, which, target):
        return send(kind, h, which, kv_buf.at[held, which, h], target)

    def wait_for(kind, h, which):
        own_send(kind, h, which, sibling).wait_recv()

    def arrived(kind, h):
        for which in range(2):
            wait_for(kind, h, which)

    barrier = pltpu.get_barrier_semaphore()
    peers = (sibling, across, along_to, along_from)
    for device in peers:
        pl.semaphore_signal(barrier, inc=1, device_id={"blk": device}, device_id_type=MESH)
    pl.semaphore_wait(barrier, len(peers))

    def begin_across(h, carry):
        for which in range(2):
            own_send(ACROSS, h, which, across).start()
        return carry

    def begin(h, carry):
        for which in range(2):
            own_send(SIBLING, h, which, sibling).start()
        for which in range(3):
            load(h, which).start()
        return carry

    lax.fori_loop(0, LOOKAHEAD, begin_across, 0)
    lax.fori_loop(0, HEADS, begin, 0)

    def head_rows(h, part):
        first = pl.multiple_of(part * rows, rows)
        q = q_buf[h, pl.ds(first, rows), :]
        peak = jnp.full((rows, 128), NEG, jnp.float32)
        for j in range(5):
            raw = nt_dot(q, kv_buf[j, 0, h]) * factor
            for b in range(blocks):
                for n in range(tok // BLOCK):
                    col = j * tok + n * BLOCK
                    piece = raw[b * BLOCK : (b + 1) * BLOCK, n * BLOCK : (n + 1) * BLOCK]
                    piece = piece + bias_ref[part * blocks + b, :, col : col + BLOCK]
                    score_buf[b * BLOCK : (b + 1) * BLOCK, col : col + BLOCK] = piece
            for n in range(tok // BLOCK):
                col = j * tok + n * BLOCK
                peak = jnp.maximum(peak, score_buf[:, col : col + BLOCK])
        top = jnp.max(peak, axis=1, keepdims=True)
        mass = jnp.zeros((rows, 128), jnp.float32)
        total = jnp.zeros((rows, head), jnp.float32)
        for j in range(5):
            weights = jnp.exp2(score_buf[:, j * tok : (j + 1) * tok] - top)
            for n in range(tok // BLOCK):
                mass = mass + weights[:, n * BLOCK : (n + 1) * BLOCK]
            total = total + jnp.dot(
                weights.astype(jnp.bfloat16), kv_buf[j, 1, h], preferred_element_type=jnp.float32
            )
        result = total / jnp.sum(mass, axis=1, keepdims=True)
        heads_ref[pl.ds(first, rows), cols(h)] = result.astype(jnp.bfloat16)

    def compute(h):
        for which in range(3):
            load(h, which).wait()
        arrived(SIBLING, h)

        @pl.when(late == 0)
        def _():
            arrived(ALONG, h)

        arrived(RELAYED, h)

        def part_step(part, carry):
            head_rows(h, part)
            return carry

        lax.fori_loop(0, tok // rows, part_step, 0)

    def relay_late(h):
        for which in range(2):
            wait_for(ALONG, h, which)
            pass_on(RELAYED, ALONG, h, which, sibling).start()

    def step(i, carry):
        @pl.when((i >= 2) & (i < HEADS))
        def _():
            compute(i - 2)

        @pl.when(i < HEADS)
        def _():
            for which in range(2):
                wait_for(ACROSS, i, which)
                pass_on(ALONG, ACROSS, i, which, along_to).start()

                @pl.when(late == 0)
                def _():
                    pass_on(RELAYED, ACROSS, i, which, sibling).start()

        @pl.when(i + LOOKAHEAD < HEADS)
        def _():
            begin_across(i + LOOKAHEAD, 0)

        @pl.when((i >= 1) & (i < HEADS + 1) & (late == 1))
        def _():
            relay_late(i - 1)

        @pl.when(i >= HEADS)
        def _():
            compute(i - 2)

        return carry

    lax.fori_loop(0, HEADS + 2, step, 0)

    def finish(h, carry):
        for kind in (ACROSS, ALONG, SIBLING, RELAYED):
            for which in range(2):
                own_send(kind, h, which, sibling).wait_send()
        return carry

    lax.fori_loop(0, HEADS, finish, 0)


def attend(slabs, queries, key_rows, value_rows, bias):
    tok, feat = queries.shape
    head = feat // HEADS
    return pl.pallas_call(
        functools.partial(attend_kernel, slabs),
        out_shape=jax.ShapeDtypeStruct((tok, feat), jnp.bfloat16),
        in_specs=[pl.BlockSpec(memory_space=pl.ANY)] * 3 + [pl.BlockSpec(memory_space=pltpu.VMEM)],
        out_specs=pl.BlockSpec(memory_space=pltpu.VMEM),
        scratch_shapes=[
            pltpu.VMEM((HEADS, tok, head), jnp.bfloat16),
            pltpu.VMEM((5, 2, HEADS, tok, head), jnp.bfloat16),
            pltpu.VMEM((min(256, tok), 5 * tok), jnp.float32),
            pltpu.SemaphoreType.DMA((4, HEADS, 2)),
            pltpu.SemaphoreType.DMA((4, HEADS, 2)),
            pltpu.SemaphoreType.DMA((HEADS, 3)),
        ],
        compiler_params=pltpu.CompilerParams(
            collective_id=0, has_side_effects=True, vmem_limit_bytes=60 * 2**20
        ),
    )(queries, key_rows, value_rows, bias)


def local(slabs, groups, queries, key_rows, value_rows, block_mask, out_weight):
    per_slab = queries.shape[0] // BLOCK
    if groups == 2 and slabs == 16 and per_slab == 4 and out_weight.shape[1] % 64 == 0:
        return fused(queries, key_rows, value_rows, block_mask, out_weight.T)
    s = lax.axis_index("blk")
    c = s % 2
    y = (s // 2) % 2
    table = jnp.where(block_mask > 0, 0.0, NEG).astype(jnp.float32)
    table = table.reshape(block_mask.shape[0], 2 * RADIUS + 1, per_slab)
    back2, back1, own, next1, next2 = (table[:, d] for d in range(5))
    ordered = jnp.concatenate(
        (
            own,
            jnp.where(y == 0, next2, back2),
            jnp.where(y == 0, back2, next2),
            jnp.where(c == 0, next1, back1),
            jnp.where(c == 0, back1, next1),
        ),
        axis=1,
    )
    bias = jnp.repeat(ordered, BLOCK, axis=1)[:, None, :]
    attention = attend(slabs, queries, key_rows, value_rows, bias)
    weight = lax.all_gather(out_weight, "blk", axis=1, tiled=True)
    return jnp.dot(attention, weight, preferred_element_type=jnp.float32).astype(jnp.bfloat16)


def solution(mesh):
    in_specs = (
        P(("groups", "blk"), None),
        P(("groups", "blk"), None),
        P(("groups", "blk"), None),
        P("blk", None),
        P(None, "blk"),
    )
    out_specs = P(("groups", "blk"), None)
    body = functools.partial(local, mesh.shape["blk"], mesh.shape["groups"])
    return jax.shard_map(body, mesh=mesh, in_specs=in_specs, out_specs=out_specs, check_vma=False)
```
